768 devices in a mesh: gx: 6 (over z_hi, core), gy: 8 (over y), gz: 16 (over z_lo, x).
Axes of the slice: x: 4, y: 8, z: 12 (z_hi: 3, z_lo: 4; z = z_hi * 4 + z_lo), core: 2. Of those that a mesh axis runs over, the one named last changes fastest.
Arguments:
- wavefunctions: bfloat16 [42, 56, 112, 128], P('gx', 'gy', 'gz'), may hold values from -8 to 8, as said below
- cell_hamiltonian: bfloat16 [6, 8, 16, 343, 343], P('gx', 'gy', 'gz'), may hold values from -0.15625 to 0.15625
- projectors: bfloat16 [6, 8, 16, 8, 18, 343], P('gx', 'gy', 'gz'), may hold values from -0.3125 to 0.3125
- atom_species: int32 [12, 16, 32], P('gx', 'gy', 'gz'), may hold values from 0 to 2, as said below
- coupling: float32 [2, 18, 18], replicated, may hold values from -0.875 to 0.875
Outputs:
- filtered: bfloat16 [42, 56, 112, 128], P('gx', 'gy', 'gz')
The draws below stay inside these ranges and needn't reach their ends.
Inputs may be any that keep to these rules, and one draw needn't show every extreme that they name: `wavefunctions`: entries that stand for the same node in neighbouring blocks are equal. `atom_species`: entries that stand for the same vertex in neighbouring blocks are equal; 0 marks a vertex without an atom, k an atom of species k.
All inputs are finite; a program needn't handle non-finite values.
Results may differ from the reference program's by a relative error of at most 0.008.
Values sent between devices are 32-bit elements; how exact they have to be, the bound alone decides.
No kernel may reach another device: no remote copies, remote signals or barrier semaphores. Data moves between devices by JAX's collectives and lax.ppermute only.
A program may use at most 32 MiB of HBM per device.

```python
import jax
import jax.numpy as jnp
from jax import lax

PDEG = 6
NN = 343
CX = 1
CY = 1
CZ = 1
NW = 128
NPROJ = 18
SPECIES = 2
ORDER = 4
NDX = 7
NDY = 7
NDZ = 7
NCX = 6
NCY = 8
NCZ = 16
N_GX = 6
N_GY = 8
N_GZ = 16


def spread_blocks(values, blocks, length, dimension):
    total = values.shape[dimension]
    positions = (jnp.arange(blocks, dtype=jnp.int32)[:, None] * (length - 1) + jnp.arange(length, dtype=jnp.int32)[None, :]) % total
    return jnp.take(values, positions.reshape(-1).astype(jnp.int32), axis=dimension)


def draw_wavefunctions(key, part):
    noise_key = jax.random.fold_in(key, 11)
    shape = (NCX * PDEG, NCY * PDEG, NCZ * PDEG, NW)
    values = jax.random.normal(noise_key, shape, jnp.float32)
    values = jnp.clip(values, -8.0, 8.0)
    values = spread_blocks(values, N_GX, NDX, 0)
    values = spread_blocks(values, N_GY, NDY, 1)
    values = spread_blocks(values, N_GZ, NDZ, 2)
    return values.astype(jnp.bfloat16)


def draw_atom_species(key, part):
    raw_key = jax.random.fold_in(key, 21)
    raw = jax.random.randint(raw_key, (NCX, NCY, NCZ), 0, 2 * SPECIES + 1, jnp.int32)
    species = jnp.where(raw > SPECIES, 0, raw).astype(jnp.int32)
    species = species.at[0, 0, 0].set(SPECIES)
    species = species.at[0, 0, 1].set(0)
    species = spread_blocks(species, N_GX, CX + 1, 0)
    species = spread_blocks(species, N_GY, CY + 1, 1)
    species = spread_blocks(species, N_GZ, CZ + 1, 2)
    return species.astype(jnp.int32)


def block_scale(key, shape, shards, least, top_value):
    gain, own = 1.0, jax.random.fold_in(key, 6)
    for dim, blocks in shards:
        draws = jnp.exp(jax.random.uniform(jax.random.fold_in(own, dim), (blocks,), jnp.float32, least / len(shards), top_value / len(shards)))
        gain = gain * jnp.repeat(draws, shape[dim] // blocks).reshape([-1 if axis == dim else 1 for axis in range(len(shape))])
    return gain


def bell_draw(rng, shape, deviation, most, cuts=(), kind=jnp.bfloat16):
    entries = deviation * jax.random.normal(rng, shape, jnp.float32)
    if cuts:
        entries = entries * block_scale(rng, shape, cuts, -0.22, 0.18)
    return jnp.clip(entries, -most, most).astype(kind)


def setup_inputs(seed: int = 0) -> dict:
    streams_of = jax.random.split(jax.random.key(seed), 6)
    wavefunctions = draw_wavefunctions(jax.random.fold_in(streams_of[5], 71), 0)
    cell_hamiltonian = bell_draw(streams_of[1], (NCX, NCY, NCZ, NN, NN), (4 * NN) ** -0.5, 0.15625, ((0, 6), (1, 8), (2, 16)))
    projectors = bell_draw(streams_of[2], (NCX, NCY, NCZ, 8, NPROJ, NN), NN ** -0.5, 0.3125, ((0, 6), (1, 8), (2, 16)))
    atom_species = draw_atom_species(jax.random.fold_in(streams_of[5], 71), 0)
    coupling = bell_draw(streams_of[4], (SPECIES, NPROJ, NPROJ), 0.15, 0.875, (), jnp.float32)
    return dict(wavefunctions=wavefunctions, cell_hamiltonian=cell_hamiltonian, projectors=projectors, atom_species=atom_species, coupling=coupling)


CENTER = 0.1
HALF = 2.0


def owned_part(values, blocks, length, dimension):
    shape = values.shape
    split = values.reshape(shape[:dimension] + (blocks, length) + shape[dimension + 1:])
    kept = lax.slice_in_dim(split, 0, length - 1, axis=dimension + 1)
    return kept.reshape(shape[:dimension] + (blocks * (length - 1),) + shape[dimension + 1:])


def block_layout(values, blocks, length, dimension):
    total = values.shape[dimension]
    positions = (jnp.arange(blocks, dtype=jnp.int32)[:, None] * (length - 1) + jnp.arange(length, dtype=jnp.int32)[None, :]) % total
    return jnp.take(values, positions.reshape(-1).astype(jnp.int32), axis=dimension)


def cell_windows(values, number, degree, dimension):
    shape = values.shape
    split = values.reshape(shape[:dimension] + (number, degree) + shape[dimension + 1:])
    following = jnp.roll(lax.slice_in_dim(split, 0, 1, axis=dimension + 1), -1, axis=dimension)
    return jnp.concatenate([split, following], axis=dimension + 1)


def cell_sums(values, dimension):
    number = values.shape[dimension]
    degree = values.shape[dimension + 1] - 1
    main_part = lax.slice_in_dim(values, 0, degree, axis=dimension + 1)
    last_row = jnp.roll(lax.slice_in_dim(values, degree, degree + 1, axis=dimension + 1), 1, axis=dimension)
    first_row = lax.slice_in_dim(main_part, 0, 1, axis=dimension + 1) + last_row
    rest_rows = lax.slice_in_dim(main_part, 1, degree, axis=dimension + 1)
    merged = jnp.concatenate([first_row, rest_rows], axis=dimension + 1)
    shape = merged.shape
    return merged.reshape(shape[:dimension] + (number * degree,) + shape[dimension + 2:])


def slab_cells(slab):
    windows = cell_windows(slab, NCY, PDEG, 1)
    windows = cell_windows(windows, NCZ, PDEG, 3)
    windows = jnp.transpose(windows, (1, 3, 0, 2, 4, 5))
    return windows.reshape(NCY, NCZ, NN, NW)


def correlation_slab(inputs):
    slab, beta = inputs
    cells = slab_cells(slab).astype(jnp.float32)
    partial_value = jnp.einsum('yzkpn,yznw->yzkpw', beta.astype(jnp.float32), cells)
    partial_value = partial_value.reshape(NCY, NCZ, 2, 2, 2, NPROJ, NW)
    summed = jnp.zeros((NCY, NCZ, 2, NPROJ, NW), jnp.float32)
    for corner_y in range(2):
        for corner_z in range(2):
            moved = jnp.roll(partial_value[:, :, :, corner_y, corner_z], corner_y, axis=0)
            summed = summed + jnp.roll(moved, corner_z, axis=1)
    return summed


def operator_slab(inputs):
    slab, hamiltonian, beta, coef_here, coef_next = inputs
    cells = slab_cells(slab).astype(jnp.float32)
    local_terms = jnp.einsum('yznm,yzmw->yznw', hamiltonian.astype(jnp.float32), cells)
    corner_list = []
    for pair in (coef_here, coef_next):
        for corner_y in range(2):
            for corner_z in range(2):
                corner_list.append(jnp.roll(jnp.roll(pair, -corner_y, axis=0), -corner_z, axis=1))
    corner_coefs = jnp.stack(corner_list, axis=2).astype(jnp.float32)
    projector_terms = jnp.einsum('yzkpn,yzkpw->yznw', beta.astype(jnp.float32), corner_coefs)
    totals = (local_terms + projector_terms).reshape(NCY, NCZ, PDEG + 1, PDEG + 1, PDEG + 1, NW)
    totals = jnp.transpose(totals, (2, 0, 3, 1, 4, 5))
    totals = cell_sums(totals, 3)
    return cell_sums(totals, 1)


def apply_operator(current, cell_hamiltonian, projectors, vertex_mask, coupling):
    slabs = cell_windows(current, NCX, PDEG, 0)
    pieces = lax.map(correlation_slab, (slabs, projectors))
    correlations = pieces[:, :, :, 0] + jnp.roll(pieces[:, :, :, 1], 1, axis=0)
    coefficients = jnp.einsum('xyzs,spq,xyzqw->xyzpw', vertex_mask, coupling, correlations, precision=lax.Precision.HIGHEST).astype(jnp.bfloat16)
    coef_next = jnp.roll(coefficients, -1, axis=0)
    terms = lax.map(operator_slab, (slabs, cell_hamiltonian, projectors, coefficients, coef_next))
    return cell_sums(terms, 0)


def reference(wavefunctions, cell_hamiltonian, projectors, atom_species, coupling):
    current = owned_part(wavefunctions, N_GX, NDX, 0)
    current = owned_part(current, N_GY, NDY, 1)
    current = owned_part(current, N_GZ, NDZ, 2)
    species = owned_part(atom_species, N_GX, CX + 1, 0)
    species = owned_part(species, N_GY, CY + 1, 1)
    species = owned_part(species, N_GZ, CZ + 1, 2)
    kinds = jnp.arange(1, SPECIES + 1, dtype=jnp.int32)
    vertex_mask = (species[..., None] == kinds).astype(jnp.float32)
    previous = current
    for step in range(ORDER):
        applied = apply_operator(current, cell_hamiltonian, projectors, vertex_mask, coupling)
        current_wide = current.astype(jnp.float32)
        if step == 0:
            updated = (applied - CENTER * current_wide) / HALF
        else:
            updated = 2.0 * (applied - CENTER * current_wide) / HALF - previous.astype(jnp.float32)
        previous = current
        current = updated.astype(jnp.bfloat16)
    result = block_layout(current, N_GX, NDX, 0)
    result = block_layout(result, N_GY, NDY, 1)
    return block_layout(result, N_GZ, NDZ, 2)
```

```python
import jax
import jax.numpy as jnp
from jax import lax
from jax.sharding import PartitionSpec as P

PDEG = 6
ORDER = 4

CENTER = 0.1
HALF = 2.0

AXES = ("gx", "gy", "gz")
FIRST = (1, 0, 0)
SECOND = (0, 1, 1)
RELATIVE = [(x, y, z) for x in range(2) for y in range(2) for z in range(2)]


def bricks(sizes, offsets):
    groups = []
    for i in range(0, sizes[0], 2):
        for j in range(0, sizes[1], 2):
            for k in range(0, sizes[2], 2):
                members = []
                for a, b, c in RELATIVE:
                    x = (i + a + offsets[0]) % sizes[0]
                    y = (j + b + offsets[1]) % sizes[1]
                    z = (k + c + offsets[2]) % sizes[2]
                    members.append((x * sizes[1] + y) * sizes[2] + z)
                groups.append(members)
    return groups


def brick_exchange(chunks, offsets, rows):
    sizes = [lax.axis_size(axis) for axis in AXES]
    bits = [(lax.axis_index(axis) + sizes[d] - offsets[d]) % 2 for d, axis in enumerate(AXES)]
    me = 4 * bits[0] + 2 * bits[1] + bits[2]
    stacked = jnp.stack([jnp.pad(c, ((0, rows - c.shape[0]), (0, 0))) for c in chunks])
    ordered = jnp.stack([lax.dynamic_index_in_dim(stacked, me ^ t, 0, keepdims=False) for t in range(8)])
    arrived = lax.all_to_all(ordered, AXES, 0, 0, axis_index_groups=bricks(sizes, offsets))
    return [
        lax.dynamic_index_in_dim(arrived, me ^ r, 0, keepdims=False)[: chunks[r].shape[0]] for r in range(8)
    ]


def side_slice(values, relative, index):
    for d in range(3):
        if relative[d]:
            values = lax.slice_in_dim(values, index, index + 1, axis=d)
    return values


def side_rows(values, relative, index):
    part = side_slice(values, relative, index)
    return part.reshape(-1, values.shape[-1])


def side_place(rows, relative, index, shape):
    part_shape = tuple(1 if d < 3 and relative[d] else n for d, n in enumerate(shape))
    part = rows.reshape(part_shape)
    pads = [
        (index, shape[d] - 1 - index, 0) if d < 3 and relative[d] else (0, 0, 0) for d in range(len(shape))
    ]
    return lax.pad(part, jnp.zeros((), rows.dtype), pads)


def brick_sum(values, offsets, index, rows):
    chunks = [side_rows(values, r, index) for r in RELATIVE]
    chunks[0] = jnp.zeros((8, values.shape[-1]), values.dtype)
    arrived = brick_exchange(chunks, offsets, rows)
    total = values
    for r, part in zip(RELATIVE[1:], arrived[1:]):
        total = total + side_place(part, r, index, values.shape)
    return total


def mirrored(values, flips):
    for d in range(3):
        values = jnp.where(flips[d], jnp.flip(values, d), values)
    return values


def exact_dot(a, b, dims):
    return lax.dot_general(a, b, (dims, ((), ())), preferred_element_type=jnp.float32).astype(a.dtype)


def local(wavefunctions, cell_hamiltonian, projectors, atom_species, coupling):
    node_count = cell_hamiltonian.shape[3]
    side = PDEG + 1
    width = wavefunctions.shape[3]
    nproj = projectors.shape[4]
    sizes = [lax.axis_size(axis) for axis in AXES]
    flips = [
        ((lax.axis_index(axis) + sizes[d] - FIRST[d]) % 2) == 1 for d, axis in enumerate(AXES)
    ]
    node = lax.broadcasted_iota(jnp.int32, (node_count, node_count), 0)
    other = lax.broadcasted_iota(jnp.int32, (node_count, node_count), 1)
    place = [node // (side * side), (node // side) % side, node % side]
    place = [jnp.where(f, side - 1 - p, p) for f, p in zip(flips, place)]
    mirror = (other == (place[0] * side + place[1]) * side + place[2]).astype(jnp.bfloat16)

    hamiltonian = cell_hamiltonian.reshape(node_count, node_count)
    hamiltonian = exact_dot(exact_dot(mirror, hamiltonian, ((1,), (0,))), mirror, ((1,), (0,)))
    betas = mirrored(projectors.reshape(2, 2, 2, nproj, node_count), flips).reshape(8 * nproj, node_count)
    betas = exact_dot(betas, mirror, ((1,), (0,)))
    start = exact_dot(mirror, wavefunctions.reshape(node_count, width), ((1,), (0,)))

    kinds = jnp.arange(1, coupling.shape[0] + 1, dtype=jnp.int32)
    species_mask = (mirrored(atom_species, flips)[..., None] == kinds).astype(jnp.float32)
    vertex_coupling = jnp.einsum(
        "xyzs,spq->xyzpq", species_mask, coupling, precision=lax.Precision.HIGHEST
    )

    current = start
    previous = start
    for step in range(ORDER):
        partial_value = jnp.dot(betas, current, preferred_element_type=jnp.float32)
        partial_value = partial_value.reshape(2, 2, 2, nproj, width)
        correlations = brick_sum(partial_value, FIRST, 1, 4 * nproj)
        correlations = brick_sum(correlations, SECOND, 0, 4 * nproj)
        coefficients = jnp.einsum(
            "xyzpq,xyzqw->xyzpw", vertex_coupling, correlations, precision=lax.Precision.HIGHEST
        ).astype(jnp.bfloat16)
        terms = jnp.dot(hamiltonian, current, preferred_element_type=jnp.float32)
        terms = terms + lax.dot_general(
            betas,
            coefficients.reshape(8 * nproj, width),
            (((0,), (0,)), ((), ())),
            preferred_element_type=jnp.float32,
        )
        terms = terms.reshape(side, side, side, width)
        applied = brick_sum(terms, SECOND, 0, 56)
        applied = brick_sum(applied, FIRST, side - 1, 56).reshape(node_count, width)
        current_wide = current.astype(jnp.float32)
        if step == 0:
            updated = (applied - CENTER * current_wide) / HALF
        else:
            updated = 2.0 * (applied - CENTER * current_wide) / HALF - previous.astype(jnp.float32)
        previous = current
        current = updated.astype(jnp.bfloat16)
    return exact_dot(mirror, current, ((1,), (0,))).reshape(wavefunctions.shape)


def solution(mesh):
    placed = (
        P("gx", "gy", "gz", None),
        P("gx", "gy", "gz", None, None),
        P("gx", "gy", "gz", None, None, None),
        P("gx", "gy", "gz"),
        P(),
    )
    return jax.shard_map(
        local, mesh=mesh, in_specs=placed, out_specs=P("gx", "gy", "gz", None), check_vma=False
    )
```

```python
import functools

import jax
import jax.numpy as jnp
import numpy as np
from jax import lax
from jax.experimental import pallas as pl
from jax.experimental.pallas import tpu as pltpu
from jax.sharding import PartitionSpec as P

PDEG = 6
ORDER = 4

CENTER = 0.1
HALF = 2.0

INTERPRET = False

SIDE = PDEG + 1
ROW = 8
NODES = SIDE * SIDE * ROW
NP = 18
CP = 8 * NP
W = 128
CHUNK = 128
FACE = 72
EDGE = 112
LAST = 127

AXES = ("gx", "gy", "gz")
OFFSETS = {1: (1, 0, 0), 0: (0, 1, 1)}
RELATIVE = [(x, y, z) for x in range(2) for y in range(2) for z in range(2)]


def bricks(sizes, offsets):
    groups = []
    for i in range(0, sizes[0], 2):
        for j in range(0, sizes[1], 2):
            for k in range(0, sizes[2], 2):
                members = []
                for a, b, c in RELATIVE:
                    x = (i + a + offsets[0]) % sizes[0]
                    y = (j + b + offsets[1]) % sizes[1]
                    z = (k + c + offsets[2]) % sizes[2]
                    members.append((x * sizes[1] + y) * sizes[2] + z)
                groups.append(members)
    return groups


def swap(chunks, side):
    sizes = [lax.axis_size(axis) for axis in AXES]
    return lax.all_to_all(chunks, AXES, 0, 0, axis_index_groups=bricks(sizes, OFFSETS[side]))


def shared(r, side):
    return [v for v, e in enumerate(RELATIVE) if all(e[d] == side for d in range(3) if RELATIVE[r][d])]


def near(r, side):
    return [v for v, e in enumerate(RELATIVE) if any(e[d] == side for d in range(3) if RELATIVE[r][d])]


def runs(corners):
    out = []
    for k, v in enumerate(corners):
        if out and out[-1][1] + out[-1][2] == NP * v:
            out[-1][2] += NP
        else:
            out.append([NP * k, NP * v, NP])
    return out


def face_nodes(r, side):
    x, y, z = RELATIVE[r]
    f = PDEG * side
    out = np.full(64, -1, np.int32)

    def row(a, b, c):
        return (a * SIDE + b) * ROW + c

    free = [d for d in range(3) if not RELATIVE[r][d]]
    if len(free) == 2:
        for i in range(SIDE):
            for j in range(SIDE):
                at = [f, f, f]
                at[free[0]], at[free[1]] = i, j
                out[8 * i + j] = row(*at)
    elif len(free) == 1:
        for i in range(SIDE):
            at = [f, f, f]
            at[free[0]] = i
            out[i] = row(*at)
    else:
        out[0] = row(f, f, f)
    return out


@functools.cache
def lane_tables(side):
    low = np.full((8, 128), -1, np.int32)
    high = np.full((8, 128), -1, np.int32)
    for r in range(1, 8):
        low[r, :64] = face_nodes(r, side)
        high[r, 64:] = face_nodes(r, side)
    return low, high


@functools.cache
def corner_table(side):
    table = np.full((CP + 7 * CHUNK, 8), -1, np.int32)

    def fill(first, lattice):
        for s, bits in enumerate(RELATIVE):
            corner = [2 * side - u if bit else u for u, bit in zip(lattice, bits)]
            if all(c in (0, 1) for c in corner):
                v = 4 * corner[0] + 2 * corner[1] + corner[2]
                table[first : first + NP, s] = NP * v + np.arange(NP)

    for v, e in enumerate(RELATIVE):
        fill(NP * v, e)
    for r in range(1, 8):
        for k, v in enumerate(near(r, side)):
            lattice = [2 * side - e if bit else e for e, bit in zip(RELATIVE[v], RELATIVE[r])]
            fill(CP + (r - 1) * CHUNK + NP * k, lattice)
    return table


def node_masks(side):
    masks = np.ones((8, NODES), np.float32)
    for r in range(1, 8):
        nodes = face_nodes(r, side)
        masks[r, nodes[nodes >= 0]] = 0.0
    return masks


def add_faces(ref, part, r, side, face=FACE, edge=EDGE, last=LAST):
    f = PDEG * side
    if r == 4:
        rows = pl.ds(f * SIDE * ROW, SIDE * ROW)
        ref[rows, :] = ref[rows, :] + part(face, SIDE * ROW)
    elif r == 2:
        for a in range(SIDE):
            rows = pl.ds((a * SIDE + f) * ROW, ROW)
            ref[rows, :] = ref[rows, :] + part(face + ROW * a, ROW)
    elif r == 1:
        rows = pl.ds(f, SIDE * SIDE, ROW)
        ref[rows, :] = ref[rows, :] + part(face, SIDE * SIDE)
    elif r == 6:
        rows = pl.ds((f * SIDE + f) * ROW, ROW)
        ref[rows, :] = ref[rows, :] + part(edge, ROW)
    elif r == 5:
        rows = pl.ds(f * SIDE * ROW + f, SIDE, ROW)
        ref[rows, :] = ref[rows, :] + part(edge, SIDE)
    elif r == 3:
        rows = pl.ds(f * ROW + f, SIDE, SIDE * ROW)
        ref[rows, :] = ref[rows, :] + part(edge, SIDE)
    else:
        rows = pl.ds((f * SIDE + f) * ROW + f, 1)
        ref[rows, :] = ref[rows, :] + part(last, 1)


def put_faces(ref, put, r, side, face=FACE, edge=EDGE, last=LAST):
    f = PDEG * side
    if r == 4:
        put(face, SIDE * ROW, ref[pl.ds(f * SIDE * ROW, SIDE * ROW), :])
    elif r == 2:
        for a in range(SIDE):
            put(face + ROW * a, ROW, ref[pl.ds((a * SIDE + f) * ROW, ROW), :])
    elif r == 1:
        put(face, SIDE * SIDE, ref[pl.ds(f, SIDE * SIDE, ROW), :])
    elif r == 6:
        put(edge, ROW, ref[pl.ds((f * SIDE + f) * ROW, ROW), :])
    elif r == 5:
        put(edge, SIDE, ref[pl.ds(f * SIDE * ROW + f, SIDE, ROW), :])
    elif r == 3:
        put(edge, SIDE, ref[pl.ds(f * ROW + f, SIDE, SIDE * ROW), :])
    else:
        put(last, 1, ref[pl.ds((f * SIDE + f) * ROW + f, 1), :])


def loader(ref, slot):
    return lambda first, rows: ref[slot, pl.ds(first, rows), :]


def storer(ref, slot):
    def put(first, rows, value):
        ref[slot, pl.ds(first, rows), :] = value

    return put


def dot(a, b):
    if INTERPRET:
        a, b = a.astype(jnp.float32), b.astype(jnp.float32)
    return jnp.dot(a, b, preferred_element_type=jnp.float32)


def open_kernel(me_ref, beta_ref, y_ref, xl_ref, xh_ref, yl_ref, yh_ref, p_ref, sx_ref, sy_ref):
    me = me_ref[0]
    p_ref[...] = dot(beta_ref[...], y_ref[...])
    row = lax.broadcasted_iota(jnp.int32, (NODES, 128), 0)
    zeros = jnp.zeros((FACE, W), jnp.float32)
    sx_ref[me] = jnp.zeros((2 * FACE, W), jnp.float32)
    sy_ref[7 - me] = zeros
    for r in range(1, 8):
        slot = me ^ r
        for first, at, rows in runs(shared(r, 1)):
            sx_ref[slot, pl.ds(first, rows), :] = p_ref[pl.ds(at, rows), :]
        used = NP * len(shared(r, 1))
        if used < FACE:
            sx_ref[slot, pl.ds(used, FACE - used), :] = jnp.zeros((FACE - used, W), jnp.float32)
        for low_ref, high_ref, out_ref, to, first in (
            (xl_ref, xh_ref, sx_ref, slot, FACE),
            (yl_ref, yh_ref, sy_ref, (7 - me) ^ r, 0),
        ):
            low = (row == low_ref[pl.ds(r, 1), :]).astype(jnp.float32).astype(jnp.bfloat16)
            high = (row == high_ref[pl.ds(r, 1), :]).astype(jnp.float32).astype(jnp.bfloat16)
            packed = dot(beta_ref[pl.ds(0, FACE), :], low) + dot(beta_ref[pl.ds(FACE, FACE), :], high)
            out_ref[to, pl.ds(first, FACE), :] = packed


def assemble_kernel(first, flip, me_ref, in_ref, beta_ref, low_ref, high_ref, table_ref, mask_ref, own_ref, far_ref, acc_ref):
    me = me_ref[0] ^ flip
    lane = lax.broadcasted_iota(jnp.int32, (128, NODES), 1)
    pick = lax.broadcasted_iota(jnp.int32, (CP + 7 * CHUNK, CP), 1)

    def chosen(s):
        return (pick == table_ref[:, pl.ds(s, 1)]).astype(jnp.float32).astype(jnp.bfloat16)

    acc_ref[...] = dot(chosen(0), beta_ref[...])
    for s in range(1, 8):
        packed = in_ref[me ^ s, pl.ds(first, FACE), :].astype(jnp.bfloat16)
        low = (lane == low_ref[:, pl.ds(s, 1)]).astype(jnp.float32).astype(jnp.bfloat16)
        high = (lane == high_ref[:, pl.ds(s, 1)]).astype(jnp.float32).astype(jnp.bfloat16)
        spread = jnp.concatenate([dot(packed, low), dot(packed, high)], axis=0).astype(jnp.bfloat16)
        acc_ref[...] = acc_ref[...] + dot(chosen(s), spread)
    own_ref[...] = acc_ref[pl.ds(0, CP), :].astype(jnp.bfloat16)
    for r in range(1, 8):
        block = acc_ref[pl.ds(CP + (r - 1) * CHUNK, CHUNK), :] * mask_ref[pl.ds(r, 1), :]
        far_ref[pl.ds((r - 1) * CHUNK, CHUNK), :] = block.astype(jnp.bfloat16)


def send_terms(me, corr_ref, coupling_ref, ham_ref, y, own_ref, c_ref, f_ref, send_ref):
    c_ref[...] = jnp.dot(
        coupling_ref[...], corr_ref[...], precision=lax.Precision.HIGHEST, preferred_element_type=jnp.float32
    )
    f_ref[...] = dot(ham_ref[...], y) + dot(own_ref[...], c_ref[...].astype(jnp.bfloat16))
    send_ref[me] = jnp.zeros((CHUNK, W), jnp.float32)
    for r in range(1, 8):
        slot = me ^ r
        corners = near(r, 0)
        used = NP * len(corners)
        if used != FACE:
            send_ref[slot, pl.ds(used // 8 * 8, CHUNK - used // 8 * 8), :] = jnp.zeros(
                (CHUNK - used // 8 * 8, W), jnp.float32
            )
        for first, at, rows in runs(corners):
            send_ref[slot, pl.ds(first, rows), :] = c_ref[pl.ds(at, rows), :]
        if r == 1:
            send_ref[slot, pl.ds(FACE + 48, 8), :] = jnp.zeros((8, W), jnp.float32)
        put_faces(f_ref, storer(send_ref, slot), r, 0)


def first_kernel(me_ref, in_ref, p_ref, y_ref, coupling_ref, ham_ref, own_ref, f_ref, send_ref, corr_ref, c_ref):
    me = me_ref[0]
    corr_ref[...] = p_ref[...]
    for r in range(1, 8):
        for first, at, rows in runs(shared(r, 1)):
            corr_ref[pl.ds(at, rows), :] = corr_ref[pl.ds(at, rows), :] + in_ref[me ^ r, pl.ds(first, rows), :]
    send_terms(7 - me, corr_ref, coupling_ref, ham_ref, y_ref[...], own_ref, c_ref, f_ref, send_ref)


def vertex_kernel(
    me_ref, in_ref, z_ref, ownx_ref, coupling_ref, ham_ref, owny_ref, y_ref, f_ref, send_ref, t_ref, corr_ref, c_ref
):
    me = me_ref[0]
    t_ref[...] = z_ref[...]
    for r in range(1, 8):
        add_faces(t_ref, loader(in_ref, me ^ r), r, 1)
    y = t_ref[...].astype(jnp.bfloat16)
    y_ref[...] = y
    corr_ref[...] = dot(ownx_ref[...], y)
    for r in range(1, 8):
        for first, at, rows in runs(near(r, 1)):
            corr_ref[pl.ds(at, rows), :] = corr_ref[pl.ds(at, rows), :] + in_ref[me ^ r, pl.ds(first, rows), :]
    send_terms(7 - me, corr_ref, coupling_ref, ham_ref, y, owny_ref, c_ref, f_ref, send_ref)


def node_kernel(scales, final, me_ref, in_ref, f_ref, fary_ref, y_ref, before_ref, share_ref, farx_ref, z_ref, send_ref, a_ref, t_ref):
    me = me_ref[0]
    for r in range(1, 8):
        a_ref[pl.ds((r - 1) * CHUNK, CHUNK), :] = in_ref[(7 - me) ^ r].astype(jnp.bfloat16)
    t_ref[...] = f_ref[...] + dot(fary_ref[...], a_ref[...])
    for r in range(1, 8):
        add_faces(t_ref, loader(in_ref, (7 - me) ^ r), r, 0)
    applied, now, before = scales
    kept = now * y_ref[...].astype(jnp.float32)
    if before:
        kept = kept + before * before_ref[...].astype(jnp.float32)
    z_ref[...] = applied * t_ref[...] + share_ref[...] * kept
    if final:
        send_ref[...] = jnp.zeros_like(send_ref)
        for r in range(1, 8):
            put_faces(z_ref, storer(send_ref, me ^ r), r, 1, 0, 0, 0)
        return
    z = z_ref[...].astype(jnp.bfloat16)
    send_ref[me] = jnp.zeros((CHUNK, W), jnp.float32)
    for r in range(1, 8):
        send_ref[me ^ r] = dot(farx_ref[pl.ds((r - 1) * CHUNK, CHUNK), :], z)
        put_faces(z_ref, storer(send_ref, me ^ r), r, 1)


def close_kernel(me_ref, in_ref, z_ref, mirror_ref, out_ref, t_ref):
    me = me_ref[0]
    t_ref[...] = z_ref[...]
    for r in range(1, 8):
        add_faces(t_ref, loader(in_ref, me ^ r), r, 1, 0, 0, 0)
    out_ref[...] = dot(mirror_ref[...], t_ref[...].astype(jnp.bfloat16)).astype(jnp.bfloat16)


def call(kernel, me, inputs, outs, scratch=()):
    smem = pl.BlockSpec(memory_space=pltpu.SMEM)
    vmem = pl.BlockSpec(memory_space=pltpu.VMEM)
    return pl.pallas_call(
        kernel,
        out_shape=[jax.ShapeDtypeStruct(shape, dtype) for shape, dtype in outs],
        in_specs=[smem] + [vmem] * len(inputs),
        out_specs=[vmem] * len(outs),
        scratch_shapes=[pltpu.VMEM(shape, dtype) for shape, dtype in scratch],
        interpret=INTERPRET,
    )(me, *inputs)


def mirrored(values, flips):
    for d in range(3):
        values = jnp.where(flips[d], jnp.flip(values, d), values)
    return values


def exact_dot(a, b, dims):
    return lax.dot_general(a, b, (dims, ((), ())), preferred_element_type=jnp.float32).astype(a.dtype)


def local(wavefunctions, cell_hamiltonian, projectors, atom_species, coupling):
    node_count = cell_hamiltonian.shape[3]
    sizes = [lax.axis_size(axis) for axis in AXES]
    bits = [(lax.axis_index(axis) + sizes[d] - OFFSETS[1][d]) % 2 for d, axis in enumerate(AXES)]
    flips = [bit == 1 for bit in bits]
    me = (4 * bits[0] + 2 * bits[1] + bits[2]).astype(jnp.int32).reshape(1)

    def mirror_of(shape, padded_dim):
        padded = lax.broadcasted_iota(jnp.int32, shape, padded_dim)
        plain = lax.broadcasted_iota(jnp.int32, shape, 1 - padded_dim)
        place = [padded // (SIDE * ROW), (padded // ROW) % SIDE, padded % ROW]
        inside = place[2] < SIDE
        place = [jnp.where(f, PDEG - p, p) for f, p in zip(flips, place)]
        same = plain == (place[0] * SIDE + place[1]) * SIDE + place[2]
        return jnp.logical_and(same, inside).astype(jnp.bfloat16)

    into = mirror_of((NODES, node_count), 0)
    back = mirror_of((node_count, NODES), 1)
    ham = exact_dot(into, cell_hamiltonian.reshape(node_count, node_count), ((1,), (0,)))
    ham = exact_dot(ham, back, ((1,), (0,)))
    betas = mirrored(projectors.reshape(2, 2, 2, NP, node_count), flips).reshape(CP, node_count)
    betas = exact_dot(betas, back, ((1,), (0,)))
    current = exact_dot(into, wavefunctions.reshape(node_count, W), ((1,), (0,)))

    species = mirrored(atom_species, flips).reshape(8)
    kinds = jnp.arange(1, coupling.shape[0] + 1, dtype=jnp.int32)
    mask = (species[:, None] == kinds).astype(jnp.float32)
    per_corner = jnp.einsum("vs,spq->vpq", mask, coupling, precision=lax.Precision.HIGHEST)
    blocks = jnp.tile(per_corner.reshape(CP, NP), (1, 8))
    corner_of = jnp.arange(CP) // NP
    blocks = jnp.where(corner_of[:, None] == corner_of[None, :], blocks, 0.0)

    f32, bf16 = jnp.float32, jnp.bfloat16
    (xl, xh), (yl, yh) = lane_tables(1), lane_tables(0)
    p, sx, sy = call(
        open_kernel,
        me,
        (betas, current, xl, xh, yl, yh),
        [((CP, W), f32), ((8, 2 * FACE, W), f32), ((8, FACE, W), f32)],
    )
    ax = swap(sx, 1)
    ay = swap(sy, 0)

    def assemble(side, arrived, first):
        low, high = lane_tables(side)
        return call(
            functools.partial(assemble_kernel, first, 0 if side else 7),
            me,
            (arrived, betas, low.T.copy(), high.T.copy(), corner_table(side), node_masks(side)),
            [((CP, NODES), bf16), ((7 * CHUNK, NODES), bf16)],
            [((CP + 7 * CHUNK, NODES), f32)],
        )

    ownx, farx = assemble(1, ax, FACE)
    owny, fary = assemble(0, ay, 0)
    owny, fary = owny.T, fary.T

    node = np.arange(NODES)
    place = [node // (SIDE * ROW), (node // ROW) % SIDE, node % ROW]
    share = np.prod([np.where(q == PDEG, 0.5, 1.0) for q in place], axis=0).astype(np.float32).reshape(NODES, 1)

    packet = ((8, CHUNK, W), f32)
    plane = (NODES, W)
    f, send = call(
        first_kernel, me, (ax, p, current, blocks, ham, owny), [(plane, f32), packet], [((CP, W), f32)] * 2
    )
    previous = current
    for step in range(ORDER):
        final = step == ORDER - 1
        arrived = swap(send, 0)
        scales = (1.0 / HALF, -CENTER / HALF, 0.0) if step == 0 else (2.0 / HALF, -2.0 * CENTER / HALF, -1.0)
        z, send = call(
            functools.partial(node_kernel, scales, final),
            me,
            (arrived, f, fary, current, previous, share, farx),
            [(plane, f32), ((8, 56, W), f32) if final else packet],
            [((7 * CHUNK, W), bf16), (plane, f32)],
        )
        arrived = swap(send, 1)
        if final:
            (out,) = call(close_kernel, me, (arrived, z, back), [((node_count, W), bf16)], [(plane, f32)])
            return out.reshape(wavefunctions.shape)
        previous = current
        current, f, send = call(
            vertex_kernel,
            me,
            (arrived, z, ownx, blocks, ham, owny),
            [(plane, bf16), (plane, f32), packet],
            [(plane, f32), ((CP, W), f32), ((CP, W), f32)],
        )


def solution(mesh):
    placed = (
        P("gx", "gy", "gz", None),
        P("gx", "gy", "gz", None, None),
        P("gx", "gy", "gz", None, None, None),
        P("gx", "gy", "gz"),
        P(),
    )
    return jax.shard_map(
        local, mesh=mesh, in_specs=placed, out_specs=P("gx", "gy", "gz", None), check_vma=False
    )
```

```python
import functools

import jax
import jax.numpy as jnp
import numpy as np
from jax import lax
from jax.experimental import pallas as pl
from jax.experimental.pallas import tpu as pltpu
from jax.sharding import PartitionSpec as P

PDEG = 6
ORDER = 4

CENTER = 0.1
HALF = 2.0

INTERPRET = False

SIDE = PDEG + 1
ROW = 8
NODES = SIDE * SIDE * ROW
NP = 18
CP = 8 * NP
W = 128
CHUNK = 128
FACE = 72
EDGE = 112
LAST = 127
LIMIT = 12 << 20

AXES = ("gx", "gy", "gz")
OFFSETS = {1: (1, 0, 0), 0: (0, 1, 1)}
RELATIVE = [(x, y, z) for x in range(2) for y in range(2) for z in range(2)]


def bricks(sizes, offsets):
    groups = []
    for i in range(0, sizes[0], 2):
        for j in range(0, sizes[1], 2):
            for k in range(0, sizes[2], 2):
                members = []
                for a, b, c in RELATIVE:
                    x = (i + a + offsets[0]) % sizes[0]
                    y = (j + b + offsets[1]) % sizes[1]
                    z = (k + c + offsets[2]) % sizes[2]
                    members.append((x * sizes[1] + y) * sizes[2] + z)
                groups.append(members)
    return groups


def swap(chunks, side):
    sizes = [lax.axis_size(axis) for axis in AXES]
    return lax.all_to_all(chunks, AXES, 0, 0, axis_index_groups=bricks(sizes, OFFSETS[side]))


def shared(r, side):
    return [v for v, e in enumerate(RELATIVE) if all(e[d] == side for d in range(3) if RELATIVE[r][d])]


def near(r, side):
    return [v for v, e in enumerate(RELATIVE) if any(e[d] == side for d in range(3) if RELATIVE[r][d])]


def runs(corners):
    out = []
    for k, v in enumerate(corners):
        if out and out[-1][1] + out[-1][2] == NP * v:
            out[-1][2] += NP
        else:
            out.append([NP * k, NP * v, NP])
    return out


def face_nodes(r, side):
    x, y, z = RELATIVE[r]
    f = PDEG * side
    out = np.full(64, -1, np.int32)

    def row(a, b, c):
        return (a * SIDE + b) * ROW + c

    free = [d for d in range(3) if not RELATIVE[r][d]]
    if len(free) == 2:
        for i in range(SIDE):
            for j in range(SIDE):
                at = [f, f, f]
                at[free[0]], at[free[1]] = i, j
                out[8 * i + j] = row(*at)
    elif len(free) == 1:
        for i in range(SIDE):
            at = [f, f, f]
            at[free[0]] = i
            out[i] = row(*at)
    else:
        out[0] = row(f, f, f)
    return out


@functools.cache
def lane_tables(side):
    low = np.full((8, 128), -1, np.int32)
    high = np.full((8, 128), -1, np.int32)
    for r in range(1, 8):
        low[r, :64] = face_nodes(r, side)
        high[r, 64:] = face_nodes(r, side)
    return low, high


@functools.cache
def mirror_tables():
    perm = np.zeros((8, NODES), np.int32)
    orig = np.full((8, NODES), -1, np.int32)
    corner = np.zeros((8, CP), np.int32)
    n = np.arange(NODES)
    place = [n // (SIDE * ROW), n // ROW % SIDE, n % ROW]
    real = place[2] < SIDE
    c = np.arange(CP)
    for me, bits in enumerate(RELATIVE):
        x, y, z = [PDEG - q if bit else q for q, bit in zip(place, bits)]
        perm[me] = np.where(real, (x * SIDE + y) * ROW + z, n)
        orig[me] = np.where(real, (x * SIDE + y) * SIDE + z, -1)
        corner[me] = NP * ((c % 8) ^ me) + c // 8
    return perm, orig, corner


@functools.cache
def corner_table(side):
    table = np.full((CP + 7 * CHUNK, 8), -1, np.int32)

    def fill(first, lattice):
        for s, bits in enumerate(RELATIVE):
            corner = [2 * side - u if bit else u for u, bit in zip(lattice, bits)]
            if all(c in (0, 1) for c in corner):
                v = 4 * corner[0] + 2 * corner[1] + corner[2]
                table[first : first + NP, s] = NP * v + np.arange(NP)

    for v, e in enumerate(RELATIVE):
        fill(NP * v, e)
    for r in range(1, 8):
        for k, v in enumerate(near(r, side)):
            lattice = [2 * side - e if bit else e for e, bit in zip(RELATIVE[v], RELATIVE[r])]
            fill(CP + (r - 1) * CHUNK + NP * k, lattice)
    return table


def node_masks(side):
    masks = np.ones((8, NODES), np.float32)
    for r in range(1, 8):
        nodes = face_nodes(r, side)
        masks[r, nodes[nodes >= 0]] = 0.0
    return masks


def add_faces(ref, part, r, side, face=FACE, edge=EDGE, last=LAST):
    f = PDEG * side
    if r == 4:
        rows = pl.ds(f * SIDE * ROW, SIDE * ROW)
        ref[rows, :] = ref[rows, :] + part(face, SIDE * ROW)
    elif r == 2:
        for a in range(SIDE):
            rows = pl.ds((a * SIDE + f) * ROW, ROW)
            ref[rows, :] = ref[rows, :] + part(face + ROW * a, ROW)
    elif r == 1:
        rows = pl.ds(f, SIDE * SIDE, ROW)
        ref[rows, :] = ref[rows, :] + part(face, SIDE * SIDE)
    elif r == 6:
        rows = pl.ds((f * SIDE + f) * ROW, ROW)
        ref[rows, :] = ref[rows, :] + part(edge, ROW)
    elif r == 5:
        rows = pl.ds(f * SIDE * ROW + f, SIDE, ROW)
        ref[rows, :] = ref[rows, :] + part(edge, SIDE)
    elif r == 3:
        rows = pl.ds(f * ROW + f, SIDE, SIDE * ROW)
        ref[rows, :] = ref[rows, :] + part(edge, SIDE)
    else:
        rows = pl.ds((f * SIDE + f) * ROW + f, 1)
        ref[rows, :] = ref[rows, :] + part(last, 1)


def put_faces(ref, put, r, side, face=FACE, edge=EDGE, last=LAST):
    f = PDEG * side
    if r == 4:
        put(face, SIDE * ROW, ref[pl.ds(f * SIDE * ROW, SIDE * ROW), :])
    elif r == 2:
        for a in range(SIDE):
            put(face + ROW * a, ROW, ref[pl.ds((a * SIDE + f) * ROW, ROW), :])
    elif r == 1:
        put(face, SIDE * SIDE, ref[pl.ds(f, SIDE * SIDE, ROW), :])
    elif r == 6:
        put(edge, ROW, ref[pl.ds((f * SIDE + f) * ROW, ROW), :])
    elif r == 5:
        put(edge, SIDE, ref[pl.ds(f * SIDE * ROW + f, SIDE, ROW), :])
    elif r == 3:
        put(edge, SIDE, ref[pl.ds(f * ROW + f, SIDE, SIDE * ROW), :])
    else:
        put(last, 1, ref[pl.ds((f * SIDE + f) * ROW + f, 1), :])


def loader(ref, slot):
    return lambda first, rows: ref[slot, pl.ds(first, rows), :]


def storer(ref, slot):
    def put(first, rows, value):
        ref[slot, pl.ds(first, rows), :] = value

    return put


def dot(a, b):
    if INTERPRET:
        a, b = a.astype(jnp.float32), b.astype(jnp.float32)
    return jnp.dot(a, b, preferred_element_type=jnp.float32)


def one_hot(mask):
    return mask.astype(jnp.float32).astype(jnp.bfloat16)


def mirror_in(me, perm_ref):
    row = lax.broadcasted_iota(jnp.int32, (NODES, NODES), 0)
    return one_hot(row == perm_ref[pl.ds(me, 1), :])


def open_kernel(
    me_ref, proj_ref, wave_ref, perm_ref, orig_ref, corner_ref, xl_ref, xh_ref, yl_ref, yh_ref,
    beta_ref, y_ref, p_ref, sx_ref, sy_ref, t_ref,
):
    me = me_ref[0]
    t_ref[...] = jnp.zeros_like(t_ref)
    for a in range(SIDE):
        for b in range(SIDE):
            t_ref[pl.ds((a * SIDE + b) * ROW, SIDE), :] = wave_ref[a, b].astype(jnp.float32)
    y_ref[...] = dot(mirror_in(me, perm_ref), t_ref[...].astype(jnp.bfloat16)).astype(jnp.bfloat16)
    flat = proj_ref[...].reshape(CP, proj_ref.shape[2])
    spread = one_hot(lax.broadcasted_iota(jnp.int32, (flat.shape[1], NODES), 0) == orig_ref[pl.ds(me, 1), :])
    order = one_hot(lax.broadcasted_iota(jnp.int32, (CP, CP), 0) == corner_ref[pl.ds(me, 1), :])
    ordered = dot(order, flat).astype(jnp.bfloat16)
    beta_ref[...] = dot(ordered, spread).astype(jnp.bfloat16)
    p_ref[...] = dot(beta_ref[...], y_ref[...])
    row = lax.broadcasted_iota(jnp.int32, (NODES, 128), 0)
    zeros = jnp.zeros((FACE, W), jnp.float32)
    sx_ref[me] = jnp.zeros((2 * FACE, W), jnp.float32)
    sy_ref[7 - me] = zeros
    for r in range(1, 8):
        slot = me ^ r
        for first, at, rows in runs(shared(r, 1)):
            sx_ref[slot, pl.ds(first, rows), :] = p_ref[pl.ds(at, rows), :]
        used = NP * len(shared(r, 1))
        if used < FACE:
            sx_ref[slot, pl.ds(used, FACE - used), :] = jnp.zeros((FACE - used, W), jnp.float32)
        for low_ref, high_ref, out_ref, to, first in (
            (xl_ref, xh_ref, sx_ref, slot, FACE),
            (yl_ref, yh_ref, sy_ref, (7 - me) ^ r, 0),
        ):
            low = one_hot(row == low_ref[pl.ds(r, 1), :])
            high = one_hot(row == high_ref[pl.ds(r, 1), :])
            packed = dot(beta_ref[pl.ds(0, FACE), :], low) + dot(beta_ref[pl.ds(FACE, FACE), :], high)
            out_ref[to, pl.ds(first, FACE), :] = packed


def assemble_kernel(first, flip, me_ref, in_ref, beta_ref, low_ref, high_ref, table_ref, mask_ref, own_ref, far_ref, acc_ref):
    me = me_ref[0] ^ flip
    lane = lax.broadcasted_iota(jnp.int32, (128, NODES), 1)
    pick = lax.broadcasted_iota(jnp.int32, (CP + 7 * CHUNK, CP), 1)

    def chosen(s):
        return (pick == table_ref[:, pl.ds(s, 1)]).astype(jnp.float32).astype(jnp.bfloat16)

    acc_ref[...] = dot(chosen(0), beta_ref[...])
    for s in range(1, 8):
        packed = in_ref[me ^ s, pl.ds(first, FACE), :].astype(jnp.bfloat16)
        low = (lane == low_ref[:, pl.ds(s, 1)]).astype(jnp.float32).astype(jnp.bfloat16)
        high = (lane == high_ref[:, pl.ds(s, 1)]).astype(jnp.float32).astype(jnp.bfloat16)
        spread = jnp.concatenate([dot(packed, low), dot(packed, high)], axis=0).astype(jnp.bfloat16)
        acc_ref[...] = acc_ref[...] + dot(chosen(s), spread)
    own_ref[...] = acc_ref[pl.ds(0, CP), :].astype(jnp.bfloat16)
    for r in range(1, 8):
        block = acc_ref[pl.ds(CP + (r - 1) * CHUNK, CHUNK), :] * mask_ref[pl.ds(r, 1), :]
        far_ref[pl.ds((r - 1) * CHUNK, CHUNK), :] = block.astype(jnp.bfloat16)


def send_terms(me, corr_ref, coupling_ref, ham_ref, y, own_ref, c_ref, f_ref, send_ref):
    c_ref[...] = jnp.dot(
        coupling_ref[...], corr_ref[...], precision=lax.Precision.HIGHEST, preferred_element_type=jnp.float32
    )
    f_ref[...] = dot(ham_ref[...], y) + dot(own_ref[...], c_ref[...].astype(jnp.bfloat16))
    send_ref[me] = jnp.zeros((CHUNK, W), jnp.float32)
    for r in range(1, 8):
        slot = me ^ r
        corners = near(r, 0)
        used = NP * len(corners)
        if used != FACE:
            send_ref[slot, pl.ds(used // 8 * 8, CHUNK - used // 8 * 8), :] = jnp.zeros(
                (CHUNK - used // 8 * 8, W), jnp.float32
            )
        for first, at, rows in runs(corners):
            send_ref[slot, pl.ds(first, rows), :] = c_ref[pl.ds(at, rows), :]
        if r == 1:
            send_ref[slot, pl.ds(FACE + 48, 8), :] = jnp.zeros((8, W), jnp.float32)
        put_faces(f_ref, storer(send_ref, slot), r, 0)


def first_kernel(me_ref, in_ref, p_ref, y_ref, coupling_ref, ham_ref, own_ref, f_ref, send_ref, corr_ref, c_ref):
    me = me_ref[0]
    corr_ref[...] = p_ref[...]
    for r in range(1, 8):
        for first, at, rows in runs(shared(r, 1)):
            corr_ref[pl.ds(at, rows), :] = corr_ref[pl.ds(at, rows), :] + in_ref[me ^ r, pl.ds(first, rows), :]
    send_terms(7 - me, corr_ref, coupling_ref, ham_ref, y_ref[...], own_ref, c_ref, f_ref, send_ref)


def vertex_kernel(
    me_ref, in_ref, z_ref, ownx_ref, coupling_ref, ham_ref, owny_ref, y_ref, f_ref, send_ref, t_ref, corr_ref, c_ref
):
    me = me_ref[0]
    t_ref[...] = z_ref[...]
    for r in range(1, 8):
        add_faces(t_ref, loader(in_ref, me ^ r), r, 1)
    y = t_ref[...].astype(jnp.bfloat16)
    y_ref[...] = y
    corr_ref[...] = dot(ownx_ref[...], y)
    for r in range(1, 8):
        for first, at, rows in runs(near(r, 1)):
            corr_ref[pl.ds(at, rows), :] = corr_ref[pl.ds(at, rows), :] + in_ref[me ^ r, pl.ds(first, rows), :]
    send_terms(7 - me, corr_ref, coupling_ref, ham_ref, y, owny_ref, c_ref, f_ref, send_ref)


def node_kernel(scales, final, me_ref, in_ref, f_ref, fary_ref, y_ref, before_ref, share_ref, farx_ref, z_ref, send_ref, a_ref, t_ref):
    me = me_ref[0]
    for r in range(1, 8):
        a_ref[pl.ds((r - 1) * CHUNK, CHUNK), :] = in_ref[(7 - me) ^ r].astype(jnp.bfloat16)
    t_ref[...] = f_ref[...] + dot(fary_ref[...], a_ref[...])
    for r in range(1, 8):
        add_faces(t_ref, loader(in_ref, (7 - me) ^ r), r, 0)
    applied, now, before = scales
    kept = now * y_ref[...].astype(jnp.float32)
    if before:
        kept = kept + before * before_ref[...].astype(jnp.float32)
    z_ref[...] = applied * t_ref[...] + share_ref[...] * kept
    if final:
        send_ref[...] = jnp.zeros_like(send_ref)
        for r in range(1, 8):
            put_faces(z_ref, storer(send_ref, me ^ r), r, 1, 0, 0, 0)
        return
    z = z_ref[...].astype(jnp.bfloat16)
    send_ref[me] = jnp.zeros((CHUNK, W), jnp.float32)
    for r in range(1, 8):
        send_ref[me ^ r] = dot(farx_ref[pl.ds((r - 1) * CHUNK, CHUNK), :], z)
        put_faces(z_ref, storer(send_ref, me ^ r), r, 1)


def close_kernel(me_ref, in_ref, z_ref, perm_ref, out_ref, t_ref):
    me = me_ref[0]
    t_ref[...] = z_ref[...]
    for r in range(1, 8):
        add_faces(t_ref, loader(in_ref, me ^ r), r, 1, 0, 0, 0)
    y = dot(mirror_in(me, perm_ref), t_ref[...].astype(jnp.bfloat16))
    for a in range(SIDE):
        for b in range(SIDE):
            first = (a * SIDE + b) * ROW
            out_ref[a, b] = y[first : first + SIDE].astype(jnp.bfloat16)


def call(kernel, me, inputs, outs, scratch=(), limit=LIMIT):
    smem = pl.BlockSpec(memory_space=pltpu.SMEM)
    vmem = pl.BlockSpec(memory_space=pltpu.VMEM)
    return pl.pallas_call(
        kernel,
        out_shape=[jax.ShapeDtypeStruct(shape, dtype) for shape, dtype in outs],
        in_specs=[smem] + [vmem] * len(inputs),
        out_specs=[vmem] * len(outs),
        scratch_shapes=[pltpu.VMEM(shape, dtype) for shape, dtype in scratch],
        compiler_params=pltpu.CompilerParams(vmem_limit_bytes=limit),
        interpret=INTERPRET,
    )(me, *inputs)


def mirrored(values, flips):
    for d in range(3):
        values = jnp.where(flips[d], jnp.flip(values, d), values)
    return values


def exact_dot(a, b, dims):
    return lax.dot_general(a, b, (dims, ((), ())), preferred_element_type=jnp.float32).astype(a.dtype)


def local(wavefunctions, cell_hamiltonian, projectors, atom_species, coupling):
    node_count = cell_hamiltonian.shape[3]
    sizes = [lax.axis_size(axis) for axis in AXES]
    bits = [(lax.axis_index(axis) + sizes[d] - OFFSETS[1][d]) % 2 for d, axis in enumerate(AXES)]
    flips = [bit == 1 for bit in bits]
    me = (4 * bits[0] + 2 * bits[1] + bits[2]).astype(jnp.int32).reshape(1)

    def mirror_of(shape, padded_dim):
        padded = lax.broadcasted_iota(jnp.int32, shape, padded_dim)
        plain = lax.broadcasted_iota(jnp.int32, shape, 1 - padded_dim)
        place = [padded // (SIDE * ROW), (padded // ROW) % SIDE, padded % ROW]
        inside = place[2] < SIDE
        place = [jnp.where(f, PDEG - p, p) for f, p in zip(flips, place)]
        same = plain == (place[0] * SIDE + place[1]) * SIDE + place[2]
        return jnp.logical_and(same, inside).astype(jnp.bfloat16)

    into = mirror_of((NODES, node_count), 0)
    back = mirror_of((node_count, NODES), 1)
    ham = exact_dot(into, cell_hamiltonian.reshape(node_count, node_count), ((1,), (0,)))
    ham = exact_dot(ham, back, ((1,), (0,)))
    species = mirrored(atom_species, flips).reshape(8)
    kinds = jnp.arange(1, coupling.shape[0] + 1, dtype=jnp.int32)
    mask = (species[:, None] == kinds).astype(jnp.float32)
    per_corner = jnp.einsum("vs,spq->vpq", mask, coupling, precision=lax.Precision.HIGHEST)
    blocks = jnp.tile(per_corner.reshape(CP, NP), (1, 8))
    corner_of = jnp.arange(CP) // NP
    blocks = jnp.where(corner_of[:, None] == corner_of[None, :], blocks, 0.0)

    f32, bf16 = jnp.float32, jnp.bfloat16
    (xl, xh), (yl, yh) = lane_tables(1), lane_tables(0)
    perm, orig, corner = mirror_tables()
    by_row = jnp.transpose(projectors.reshape(8, NP, node_count), (1, 0, 2))
    betas, current, p, sx, sy = call(
        open_kernel,
        me,
        (by_row, wavefunctions, perm, orig, corner, xl, xh, yl, yh),
        [((CP, NODES), bf16), ((NODES, W), bf16), ((CP, W), f32), ((8, 2 * FACE, W), f32), ((8, FACE, W), f32)],
        [((NODES, W), f32)],
    )
    ax = swap(sx, 1)
    ay = swap(sy, 0)

    def assemble(side, arrived, first):
        low, high = lane_tables(side)
        return call(
            functools.partial(assemble_kernel, first, 0 if side else 7),
            me,
            (arrived, betas, low.T.copy(), high.T.copy(), corner_table(side), node_masks(side)),
            [((CP, NODES), bf16), ((7 * CHUNK, NODES), bf16)],
            [((CP + 7 * CHUNK, NODES), f32)],
        )

    ownx, farx = assemble(1, ax, FACE)
    owny, fary = assemble(0, ay, 0)
    owny, fary = owny.T, fary.T

    node = np.arange(NODES)
    place = [node // (SIDE * ROW), (node // ROW) % SIDE, node % ROW]
    share = np.prod([np.where(q == PDEG, 0.5, 1.0) for q in place], axis=0).astype(np.float32).reshape(NODES, 1)

    packet = ((8, CHUNK, W), f32)
    plane = (NODES, W)
    f, send = call(
        first_kernel, me, (ax, p, current, blocks, ham, owny), [(plane, f32), packet], [((CP, W), f32)] * 2
    )
    previous = current
    for step in range(ORDER):
        final = step == ORDER - 1
        arrived = swap(send, 0)
        scales = (1.0 / HALF, -CENTER / HALF, 0.0) if step == 0 else (2.0 / HALF, -2.0 * CENTER / HALF, -1.0)
        z, send = call(
            functools.partial(node_kernel, scales, final),
            me,
            (arrived, f, fary, current, previous, share, farx),
            [(plane, f32), ((8, 56, W), f32) if final else packet],
            [((7 * CHUNK, W), bf16), (plane, f32)],
        )
        arrived = swap(send, 1)
        if final:
            (out,) = call(close_kernel, me, (arrived, z, perm), [(wavefunctions.shape, bf16)], [(plane, f32)])
            return out
        previous = current
        current, f, send = call(
            vertex_kernel,
            me,
            (arrived, z, ownx, blocks, ham, owny),
            [(plane, bf16), (plane, f32), packet],
            [(plane, f32), ((CP, W), f32), ((CP, W), f32)],
        )


def solution(mesh):
    placed = (
        P("gx", "gy", "gz", None),
        P("gx", "gy", "gz", None, None),
        P("gx", "gy", "gz", None, None, None),
        P("gx", "gy", "gz"),
        P(),
    )
    return jax.shard_map(
        local, mesh=mesh, in_specs=placed, out_specs=P("gx", "gy", "gz", None), check_vma=False
    )
```

```python
import functools

import jax
import jax.numpy as jnp
import numpy as np
from jax import lax
from jax.experimental import pallas as pl
from jax.experimental.pallas import tpu as pltpu
from jax.sharding import PartitionSpec as P

PDEG = 6
ORDER = 4

CENTER = 0.1
HALF = 2.0

INTERPRET = False

SIDE = PDEG + 1
ROW = 8
NODES = SIDE * SIDE * ROW
NP = 18
CP = 8 * NP
W = 128
CHUNK = 128
FACE = 72
EDGE = 112
LAST = 127
FAR = 7 * CHUNK
ROWS = FAR + CP
LIMIT = 12 << 20

AXES = ("gx", "gy", "gz")
OFFSETS = {1: (1, 0, 0), 0: (0, 1, 1)}
RELATIVE = [(x, y, z) for x in range(2) for y in range(2) for z in range(2)]


def bricks(sizes, offsets):
    groups = []
    for i in range(0, sizes[0], 2):
        for j in range(0, sizes[1], 2):
            for k in range(0, sizes[2], 2):
                members = []
                for a, b, c in RELATIVE:
                    x = (i + a + offsets[0]) % sizes[0]
                    y = (j + b + offsets[1]) % sizes[1]
                    z = (k + c + offsets[2]) % sizes[2]
                    members.append((x * sizes[1] + y) * sizes[2] + z)
                groups.append(members)
    return groups


def swap(chunks, side):
    sizes = [lax.axis_size(axis) for axis in AXES]
    return lax.all_to_all(chunks, AXES, 0, 0, axis_index_groups=bricks(sizes, OFFSETS[side]))


def shared(r, side):
    return [v for v, e in enumerate(RELATIVE) if all(e[d] == side for d in range(3) if RELATIVE[r][d])]


def near(r, side):
    return [v for v, e in enumerate(RELATIVE) if any(e[d] == side for d in range(3) if RELATIVE[r][d])]


def runs(corners):
    out = []
    for k, v in enumerate(corners):
        if out and out[-1][1] + out[-1][2] == NP * v:
            out[-1][2] += NP
        else:
            out.append([NP * k, NP * v, NP])
    return out


def face_nodes(r, side):
    x, y, z = RELATIVE[r]
    f = PDEG * side
    out = np.full(64, -1, np.int32)

    def row(a, b, c):
        return (a * SIDE + b) * ROW + c

    free = [d for d in range(3) if not RELATIVE[r][d]]
    if len(free) == 2:
        for i in range(SIDE):
            for j in range(SIDE):
                at = [f, f, f]
                at[free[0]], at[free[1]] = i, j
                out[8 * i + j] = row(*at)
    elif len(free) == 1:
        for i in range(SIDE):
            at = [f, f, f]
            at[free[0]] = i
            out[i] = row(*at)
    else:
        out[0] = row(f, f, f)
    return out


@functools.cache
def lane_tables(side):
    low = np.full((8, 128), -1, np.int32)
    high = np.full((8, 128), -1, np.int32)
    for r in range(1, 8):
        low[r, :64] = face_nodes(r, side)
        high[r, 64:] = face_nodes(r, side)
    return low, high


@functools.cache
def mirror_tables():
    perm = np.zeros((8, NODES), np.int32)
    orig = np.full((8, NODES), -1, np.int32)
    corner = np.zeros((8, CP), np.int32)
    n = np.arange(NODES)
    place = [n // (SIDE * ROW), n // ROW % SIDE, n % ROW]
    real = place[2] < SIDE
    c = np.arange(CP)
    for me, bits in enumerate(RELATIVE):
        x, y, z = [PDEG - q if bit else q for q, bit in zip(place, bits)]
        perm[me] = np.where(real, (x * SIDE + y) * ROW + z, n)
        orig[me] = np.where(real, (x * SIDE + y) * SIDE + z, -1)
        corner[me] = NP * ((c % 8) ^ me) + c // 8
    return np.concatenate([perm, orig]), corner


@functools.cache
def corner_table(side):
    table = np.full((ROWS, 8), -1, np.int32)

    def fill(first, lattice):
        for s, bits in enumerate(RELATIVE):
            corner = [2 * side - u if bit else u for u, bit in zip(lattice, bits)]
            if all(c in (0, 1) for c in corner):
                v = 4 * corner[0] + 2 * corner[1] + corner[2]
                table[first : first + NP, s] = NP * v + np.arange(NP)

    for v, e in enumerate(RELATIVE):
        fill(FAR + NP * v, e)
    for r in range(1, 8):
        for k, v in enumerate(near(r, side)):
            lattice = [2 * side - e if bit else e for e, bit in zip(RELATIVE[v], RELATIVE[r])]
            fill((r - 1) * CHUNK + NP * k, lattice)
    return table.T


def add_faces(ref, part, r, side, face=FACE, edge=EDGE, last=LAST):
    f = PDEG * side
    if r == 4:
        rows = pl.ds(f * SIDE * ROW, SIDE * ROW)
        ref[rows, :] = ref[rows, :] + part(face, SIDE * ROW)
    elif r == 2:
        for a in range(SIDE):
            rows = pl.ds((a * SIDE + f) * ROW, ROW)
            ref[rows, :] = ref[rows, :] + part(face + ROW * a, ROW)
    elif r == 1:
        rows = pl.ds(f, SIDE * SIDE, ROW)
        ref[rows, :] = ref[rows, :] + part(face, SIDE * SIDE)
    elif r == 6:
        rows = pl.ds((f * SIDE + f) * ROW, ROW)
        ref[rows, :] = ref[rows, :] + part(edge, ROW)
    elif r == 5:
        rows = pl.ds(f * SIDE * ROW + f, SIDE, ROW)
        ref[rows, :] = ref[rows, :] + part(edge, SIDE)
    elif r == 3:
        rows = pl.ds(f * ROW + f, SIDE, SIDE * ROW)
        ref[rows, :] = ref[rows, :] + part(edge, SIDE)
    else:
        rows = pl.ds((f * SIDE + f) * ROW + f, 1)
        ref[rows, :] = ref[rows, :] + part(last, 1)


def put_faces(ref, put, r, side, face=FACE, edge=EDGE, last=LAST):
    f = PDEG * side
    if r == 4:
        put(face, SIDE * ROW, ref[pl.ds(f * SIDE * ROW, SIDE * ROW), :])
    elif r == 2:
        for a in range(SIDE):
            put(face + ROW * a, ROW, ref[pl.ds((a * SIDE + f) * ROW, ROW), :])
    elif r == 1:
        put(face, SIDE * SIDE, ref[pl.ds(f, SIDE * SIDE, ROW), :])
    elif r == 6:
        put(edge, ROW, ref[pl.ds((f * SIDE + f) * ROW, ROW), :])
    elif r == 5:
        put(edge, SIDE, ref[pl.ds(f * SIDE * ROW + f, SIDE, ROW), :])
    elif r == 3:
        put(edge, SIDE, ref[pl.ds(f * ROW + f, SIDE, SIDE * ROW), :])
    else:
        put(last, 1, ref[pl.ds((f * SIDE + f) * ROW + f, 1), :])


def loader(ref, slot):
    return lambda first, rows: ref[slot, pl.ds(first, rows), :]


def storer(ref, slot):
    def put(first, rows, value):
        ref[slot, pl.ds(first, rows), :] = value

    return put


def dot(a, b):
    if INTERPRET:
        a, b = a.astype(jnp.float32), b.astype(jnp.float32)
    return jnp.dot(a, b, preferred_element_type=jnp.float32)


def one_hot(mask):
    return mask.astype(jnp.float32).astype(jnp.bfloat16)


def mirror_in(me, perm_ref):
    row = lax.broadcasted_iota(jnp.int32, (NODES, NODES), 0)
    return one_hot(row == perm_ref[pl.ds(me, 1), :])


def open_kernel(
    me_ref, proj_ref, wave_ref, perm_ref, corner_ref, lane_ref, beta_ref, turned_ref, y_ref, p_ref, sx_ref, sy_ref, t_ref
):
    me = me_ref[0]
    t_ref[...] = jnp.zeros_like(t_ref)
    for a in range(SIDE):
        for b in range(SIDE):
            t_ref[pl.ds((a * SIDE + b) * ROW, SIDE), :] = wave_ref[a, b].astype(jnp.float32)
    y_ref[...] = dot(mirror_in(me, perm_ref), t_ref[...].astype(jnp.bfloat16)).astype(jnp.bfloat16)
    flat = proj_ref[...].reshape(CP, proj_ref.shape[2])
    spread = one_hot(lax.broadcasted_iota(jnp.int32, (flat.shape[1], NODES), 0) == perm_ref[pl.ds(8 + me, 1), :])
    order = one_hot(lax.broadcasted_iota(jnp.int32, (CP, CP), 0) == corner_ref[pl.ds(me, 1), :])
    ordered = dot(order, flat).astype(jnp.bfloat16)
    beta_ref[...] = dot(ordered, spread).astype(jnp.bfloat16)
    p_ref[...] = dot(beta_ref[...], y_ref[...])
    same = one_hot(lax.broadcasted_iota(jnp.int32, (NODES, NODES), 0) == lax.broadcasted_iota(jnp.int32, (NODES, NODES), 1))
    turned_ref[...] = dot_nt(same, beta_ref[...]).astype(jnp.bfloat16)
    row = lax.broadcasted_iota(jnp.int32, (NODES, 128), 0)
    zeros = jnp.zeros((FACE, W), jnp.float32)
    sx_ref[me] = jnp.zeros((2 * FACE, W), jnp.float32)
    sy_ref[7 - me] = zeros
    for r in range(1, 8):
        slot = me ^ r
        for first, at, rows in runs(shared(r, 1)):
            sx_ref[slot, pl.ds(first, rows), :] = p_ref[pl.ds(at, rows), :]
        used = NP * len(shared(r, 1))
        if used < FACE:
            sx_ref[slot, pl.ds(used, FACE - used), :] = jnp.zeros((FACE - used, W), jnp.float32)
        for base, out_ref, to, first in ((0, sx_ref, slot, FACE), (16, sy_ref, (7 - me) ^ r, 0)):
            low = one_hot(row == lane_ref[pl.ds(base + r, 1), :])
            high = one_hot(row == lane_ref[pl.ds(base + 8 + r, 1), :])
            packed = dot(beta_ref[pl.ds(0, FACE), :], low) + dot(beta_ref[pl.ds(FACE, FACE), :], high)
            out_ref[to, pl.ds(first, FACE), :] = packed


def dot_nt(a, b):
    if INTERPRET:
        a, b = a.astype(jnp.float32), b.astype(jnp.float32)
    return lax.dot_general(a, b, (((1,), (1,)), ((), ())), preferred_element_type=jnp.float32)


def dot_tn(a, b):
    if INTERPRET:
        a, b = a.astype(jnp.float32), b.astype(jnp.float32)
    return lax.dot_general(a, b, (((0,), (0,)), ((), ())), preferred_element_type=jnp.float32)


def assemble_kernel(side, first, me_ref, in_ref, beta_ref, lane_ref, table_ref, own_ref, far_ref, acc_ref):
    me = me_ref[0] if side else 7 - me_ref[0]
    base = 16 * (1 - side)
    node = lax.broadcasted_iota(jnp.int32, (NODES, 128), 0)

    def chosen(s, at, rows):
        pick = lax.broadcasted_iota(jnp.int32, (rows, ROWS), 0) + at
        return one_hot(pick == table_ref[pl.ds(8 * (1 - side) + s, 1), :])

    if side:
        acc_ref[...] = dot_tn(chosen(0, 0, CP), beta_ref[...])
    else:
        acc_ref[...] = dot(beta_ref[...], chosen(0, 0, CP))
    for s in range(1, 8):
        packed = in_ref[me ^ s, pl.ds(first, FACE), :].astype(jnp.bfloat16)
        for half in range(2):
            spread = one_hot(node == lane_ref[pl.ds(base + 8 * half + s, 1), :])
            pick = chosen(s, FACE * half, FACE)
            if side:
                term = dot_tn(pick, dot_nt(packed, spread).astype(jnp.bfloat16))
            else:
                term = dot(dot_nt(spread, packed).astype(jnp.bfloat16), pick)
            acc_ref[...] = acc_ref[...] + term
    for r in range(1, 8):
        touched = (node == lane_ref[pl.ds(base + r, 1), :]).astype(jnp.float32)
        if side:
            mask = 1.0 - lax.dot_general(
                jnp.ones((8, 128), jnp.float32), touched, (((1,), (1,)), ((), ())), preferred_element_type=jnp.float32
            )
            block = acc_ref[pl.ds((r - 1) * CHUNK, CHUNK), :] * mask[0:1, :]
            far_ref[pl.ds((r - 1) * CHUNK, CHUNK), :] = block.astype(jnp.bfloat16)
        else:
            mask = 1.0 - jnp.sum(touched, axis=1, keepdims=True)
            block = acc_ref[:, pl.ds((r - 1) * CHUNK, CHUNK)] * mask
            far_ref[:, pl.ds((r - 1) * CHUNK, CHUNK)] = block.astype(jnp.bfloat16)
    if side:
        own_ref[...] = acc_ref[pl.ds(FAR, CP), :].astype(jnp.bfloat16)
    else:
        own_ref[...] = acc_ref[:, pl.ds(FAR, CP)].astype(jnp.bfloat16)


def send_terms(me, corr_ref, coupling_ref, ham_ref, y, own_ref, c_ref, f_ref, send_ref):
    c_ref[...] = jnp.dot(
        coupling_ref[...], corr_ref[...], precision=lax.Precision.HIGHEST, preferred_element_type=jnp.float32
    )
    f_ref[...] = dot(ham_ref[...], y) + dot(own_ref[...], c_ref[...].astype(jnp.bfloat16))
    send_ref[me] = jnp.zeros((CHUNK, W), jnp.float32)
    for r in range(1, 8):
        slot = me ^ r
        corners = near(r, 0)
        used = NP * len(corners)
        if used != FACE:
            send_ref[slot, pl.ds(used // 8 * 8, CHUNK - used // 8 * 8), :] = jnp.zeros(
                (CHUNK - used // 8 * 8, W), jnp.float32
            )
        for first, at, rows in runs(corners):
            send_ref[slot, pl.ds(first, rows), :] = c_ref[pl.ds(at, rows), :]
        if r == 1:
            send_ref[slot, pl.ds(FACE + 48, 8), :] = jnp.zeros((8, W), jnp.float32)
        put_faces(f_ref, storer(send_ref, slot), r, 0)


def first_kernel(me_ref, in_ref, p_ref, y_ref, coupling_ref, ham_ref, own_ref, f_ref, send_ref, corr_ref, c_ref):
    me = me_ref[0]
    corr_ref[...] = p_ref[...]
    for r in range(1, 8):
        for first, at, rows in runs(shared(r, 1)):
            corr_ref[pl.ds(at, rows), :] = corr_ref[pl.ds(at, rows), :] + in_ref[me ^ r, pl.ds(first, rows), :]
    send_terms(7 - me, corr_ref, coupling_ref, ham_ref, y_ref[...], own_ref, c_ref, f_ref, send_ref)


def vertex_kernel(
    me_ref, in_ref, z_ref, ownx_ref, coupling_ref, ham_ref, owny_ref, y_ref, f_ref, send_ref, t_ref, corr_ref, c_ref
):
    me = me_ref[0]
    t_ref[...] = z_ref[...]
    for r in range(1, 8):
        add_faces(t_ref, loader(in_ref, me ^ r), r, 1)
    y = t_ref[...].astype(jnp.bfloat16)
    y_ref[...] = y
    corr_ref[...] = dot(ownx_ref[...], y)
    for r in range(1, 8):
        for first, at, rows in runs(near(r, 1)):
            corr_ref[pl.ds(at, rows), :] = corr_ref[pl.ds(at, rows), :] + in_ref[me ^ r, pl.ds(first, rows), :]
    send_terms(7 - me, corr_ref, coupling_ref, ham_ref, y, owny_ref, c_ref, f_ref, send_ref)


def node_kernel(scales, final, me_ref, in_ref, f_ref, fary_ref, y_ref, before_ref, share_ref, farx_ref, z_ref, send_ref, a_ref, t_ref):
    me = me_ref[0]
    for r in range(1, 8):
        a_ref[pl.ds((r - 1) * CHUNK, CHUNK), :] = in_ref[(7 - me) ^ r].astype(jnp.bfloat16)
    t_ref[...] = f_ref[...] + dot(fary_ref[...], a_ref[...])
    for r in range(1, 8):
        add_faces(t_ref, loader(in_ref, (7 - me) ^ r), r, 0)
    applied, now, before = scales
    kept = now * y_ref[...].astype(jnp.float32)
    if before:
        kept = kept + before * before_ref[...].astype(jnp.float32)
    z_ref[...] = applied * t_ref[...] + share_ref[...] * kept
    if final:
        send_ref[...] = jnp.zeros_like(send_ref)
        for r in range(1, 8):
            put_faces(z_ref, storer(send_ref, me ^ r), r, 1, 0, 0, 0)
        return
    z = z_ref[...].astype(jnp.bfloat16)
    send_ref[me] = jnp.zeros((CHUNK, W), jnp.float32)
    for r in range(1, 8):
        send_ref[me ^ r] = dot(farx_ref[pl.ds((r - 1) * CHUNK, CHUNK), :], z)
        put_faces(z_ref, storer(send_ref, me ^ r), r, 1)


def close_kernel(me_ref, in_ref, z_ref, perm_ref, out_ref, t_ref):
    me = me_ref[0]
    t_ref[...] = z_ref[...]
    for r in range(1, 8):
        add_faces(t_ref, loader(in_ref, me ^ r), r, 1, 0, 0, 0)
    y = dot(mirror_in(me, perm_ref), t_ref[...].astype(jnp.bfloat16))
    for a in range(SIDE):
        for b in range(SIDE):
            first = (a * SIDE + b) * ROW
            out_ref[a, b] = y[first : first + SIDE].astype(jnp.bfloat16)


def call(kernel, me, inputs, outs, scratch=(), limit=LIMIT):
    smem = pl.BlockSpec(memory_space=pltpu.SMEM)
    vmem = pl.BlockSpec(memory_space=pltpu.VMEM)
    return pl.pallas_call(
        kernel,
        out_shape=[jax.ShapeDtypeStruct(shape, dtype) for shape, dtype in outs],
        in_specs=[smem] + [vmem] * len(inputs),
        out_specs=[vmem] * len(outs),
        scratch_shapes=[pltpu.VMEM(shape, dtype) for shape, dtype in scratch],
        compiler_params=pltpu.CompilerParams(vmem_limit_bytes=limit),
        interpret=INTERPRET,
    )(me, *inputs)


def mirrored(values, flips):
    for d in range(3):
        values = jnp.where(flips[d], jnp.flip(values, d), values)
    return values


def exact_dot(a, b, dims):
    return lax.dot_general(a, b, (dims, ((), ())), preferred_element_type=jnp.float32).astype(a.dtype)


def local(wavefunctions, cell_hamiltonian, projectors, atom_species, coupling):
    node_count = cell_hamiltonian.shape[3]
    sizes = [lax.axis_size(axis) for axis in AXES]
    bits = [(lax.axis_index(axis) + sizes[d] - OFFSETS[1][d]) % 2 for d, axis in enumerate(AXES)]
    flips = [bit == 1 for bit in bits]
    me = (4 * bits[0] + 2 * bits[1] + bits[2]).astype(jnp.int32).reshape(1)

    def mirror_of(shape, padded_dim):
        padded = lax.broadcasted_iota(jnp.int32, shape, padded_dim)
        plain = lax.broadcasted_iota(jnp.int32, shape, 1 - padded_dim)
        place = [padded // (SIDE * ROW), (padded // ROW) % SIDE, padded % ROW]
        inside = place[2] < SIDE
        place = [jnp.where(f, PDEG - p, p) for f, p in zip(flips, place)]
        same = plain == (place[0] * SIDE + place[1]) * SIDE + place[2]
        return jnp.logical_and(same, inside).astype(jnp.bfloat16)

    into = mirror_of((NODES, node_count), 0)
    back = mirror_of((node_count, NODES), 1)
    ham = exact_dot(into, cell_hamiltonian.reshape(node_count, node_count), ((1,), (0,)))
    ham = exact_dot(ham, back, ((1,), (0,)))
    species = mirrored(atom_species, flips).reshape(8)
    kinds = jnp.arange(1, coupling.shape[0] + 1, dtype=jnp.int32)
    mask = (species[:, None] == kinds).astype(jnp.float32)
    per_corner = jnp.einsum("vs,spq->vpq", mask, coupling, precision=lax.Precision.HIGHEST)
    blocks = jnp.tile(per_corner.reshape(CP, NP), (1, 8))
    corner_of = jnp.arange(CP) // NP
    blocks = jnp.where(corner_of[:, None] == corner_of[None, :], blocks, 0.0)

    f32, bf16 = jnp.float32, jnp.bfloat16
    lanes = np.concatenate([*lane_tables(1), *lane_tables(0)])
    tables = np.concatenate([corner_table(1), corner_table(0)])
    perm, corner = mirror_tables()
    by_row = jnp.transpose(projectors.reshape(8, NP, node_count), (1, 0, 2))
    plane = (NODES, W)
    betas, turned, current, p, sx, sy = call(
        open_kernel,
        me,
        (by_row, wavefunctions, perm, corner, lanes),
        [
            ((CP, NODES), bf16),
            ((NODES, CP), bf16),
            (plane, bf16),
            ((CP, W), f32),
            ((8, 2 * FACE, W), f32),
            ((8, FACE, W), f32),
        ],
        [(plane, f32)],
        58 << 20,
    )
    ax = swap(sx, 1)
    ay = swap(sy, 0)
    ownx, farx = call(
        functools.partial(assemble_kernel, 1, FACE),
        me,
        (ax, betas, lanes, tables),
        [((CP, NODES), bf16), ((FAR, NODES), bf16)],
        [((ROWS, NODES), f32)],
    )
    owny, fary = call(
        functools.partial(assemble_kernel, 0, 0),
        me,
        (ay, turned, lanes, tables),
        [((NODES, CP), bf16), ((NODES, FAR), bf16)],
        [((NODES, ROWS), f32)],
    )

    node = np.arange(NODES)
    place = [node // (SIDE * ROW), (node // ROW) % SIDE, node % ROW]
    share = np.prod([np.where(q == PDEG, 0.5, 1.0) for q in place], axis=0).astype(np.float32).reshape(NODES, 1)

    packet = ((8, CHUNK, W), f32)
    f, send = call(
        first_kernel, me, (ax, p, current, blocks, ham, owny), [(plane, f32), packet], [((CP, W), f32)] * 2
    )
    previous = current
    for step in range(ORDER):
        final = step == ORDER - 1
        arrived = swap(send, 0)
        scales = (1.0 / HALF, -CENTER / HALF, 0.0) if step == 0 else (2.0 / HALF, -2.0 * CENTER / HALF, -1.0)
        z, send = call(
            functools.partial(node_kernel, scales, final),
            me,
            (arrived, f, fary, current, previous, share, farx),
            [(plane, f32), ((8, 56, W), f32) if final else packet],
            [((7 * CHUNK, W), bf16), (plane, f32)],
        )
        arrived = swap(send, 1)
        if final:
            (out,) = call(close_kernel, me, (arrived, z, perm), [(wavefunctions.shape, bf16)], [(plane, f32)])
            return out
        previous = current
        current, f, send = call(
            vertex_kernel,
            me,
            (arrived, z, ownx, blocks, ham, owny),
            [(plane, bf16), (plane, f32), packet],
            [(plane, f32), ((CP, W), f32), ((CP, W), f32)],
        )


def solution(mesh):
    placed = (
        P("gx", "gy", "gz", None),
        P("gx", "gy", "gz", None, None),
        P("gx", "gy", "gz", None, None, None),
        P("gx", "gy", "gz"),
        P(),
    )
    return jax.shard_map(
        local, mesh=mesh, in_specs=placed, out_specs=P("gx", "gy", "gz", None), check_vma=False
    )
```

```python
import functools

import jax
import jax.numpy as jnp
import numpy as np
from jax import lax
from jax.experimental import pallas as pl
from jax.experimental.pallas import tpu as pltpu
from jax.sharding import PartitionSpec as P

PDEG = 6
ORDER = 4

CENTER = 0.1
HALF = 2.0

INTERPRET = False

SIDE = PDEG + 1
ROW = 8
NODES = SIDE * SIDE * ROW
NP = 18
CP = 8 * NP
W = 128
CHUNK = 128
FACE = 72
EDGE = 112
LAST = 127
FAR = 7 * CHUNK
ROWS = FAR + CP
LIMIT = 12 << 20

AXES = ("gx", "gy", "gz")
OFFSETS = {1: (1, 0, 0), 0: (0, 1, 1)}
RELATIVE = [(x, y, z) for x in range(2) for y in range(2) for z in range(2)]


def bricks(sizes, offsets):
    groups = []
    for i in range(0, sizes[0], 2):
        for j in range(0, sizes[1], 2):
            for k in range(0, sizes[2], 2):
                members = []
                for a, b, c in RELATIVE:
                    x = (i + a + offsets[0]) % sizes[0]
                    y = (j + b + offsets[1]) % sizes[1]
                    z = (k + c + offsets[2]) % sizes[2]
                    members.append((x * sizes[1] + y) * sizes[2] + z)
                groups.append(members)
    return groups


def swap(chunks, side):
    sizes = [lax.axis_size(axis) for axis in AXES]
    return lax.all_to_all(chunks, AXES, 0, 0, axis_index_groups=bricks(sizes, OFFSETS[side]))


def shared(r, side):
    return [v for v, e in enumerate(RELATIVE) if all(e[d] == side for d in range(3) if RELATIVE[r][d])]


def near(r, side):
    return [v for v, e in enumerate(RELATIVE) if any(e[d] == side for d in range(3) if RELATIVE[r][d])]


def runs(corners):
    out = []
    for k, v in enumerate(corners):
        if out and out[-1][1] + out[-1][2] == NP * v:
            out[-1][2] += NP
        else:
            out.append([NP * k, NP * v, NP])
    return out


def face_nodes(r, side):
    x, y, z = RELATIVE[r]
    f = PDEG * side
    out = np.full(64, -1, np.int32)

    def row(a, b, c):
        return (a * SIDE + b) * ROW + c

    free = [d for d in range(3) if not RELATIVE[r][d]]
    if len(free) == 2:
        for i in range(SIDE):
            for j in range(SIDE):
                at = [f, f, f]
                at[free[0]], at[free[1]] = i, j
                out[8 * i + j] = row(*at)
    elif len(free) == 1:
        for i in range(SIDE):
            at = [f, f, f]
            at[free[0]] = i
            out[i] = row(*at)
    else:
        out[0] = row(f, f, f)
    return out


@functools.cache
def lane_tables(side):
    low = np.full((8, 128), -1, np.int32)
    high = np.full((8, 128), -1, np.int32)
    for r in range(1, 8):
        low[r, :64] = face_nodes(r, side)
        high[r, 64:] = face_nodes(r, side)
    return low, high


@functools.cache
def mirror_tables():
    perm = np.zeros((8, NODES), np.int32)
    orig = np.full((8, NODES), -1, np.int32)
    corner = np.zeros((8, CP), np.int32)
    n = np.arange(NODES)
    place = [n // (SIDE * ROW), n // ROW % SIDE, n % ROW]
    real = place[2] < SIDE
    c = np.arange(CP)
    for me, bits in enumerate(RELATIVE):
        x, y, z = [PDEG - q if bit else q for q, bit in zip(place, bits)]
        perm[me] = np.where(real, (x * SIDE + y) * ROW + z, n)
        orig[me] = np.where(real, (x * SIDE + y) * SIDE + z, -1)
        corner[me] = NP * ((c % 8) ^ me) + c // 8
    return np.concatenate([perm, orig]), corner


@functools.cache
def corner_table(side):
    table = np.full((ROWS, 8), -1, np.int32)

    def fill(first, lattice):
        for s, bits in enumerate(RELATIVE):
            corner = [2 * side - u if bit else u for u, bit in zip(lattice, bits)]
            if all(c in (0, 1) for c in corner):
                v = 4 * corner[0] + 2 * corner[1] + corner[2]
                table[first : first + NP, s] = NP * v + np.arange(NP)

    for v, e in enumerate(RELATIVE):
        fill(FAR + NP * v, e)
    for r in range(1, 8):
        for k, v in enumerate(near(r, side)):
            lattice = [2 * side - e if bit else e for e, bit in zip(RELATIVE[v], RELATIVE[r])]
            fill((r - 1) * CHUNK + NP * k, lattice)
    return table.T


def add_faces(ref, part, r, side, face=FACE, edge=EDGE, last=LAST):
    f = PDEG * side
    if r == 4:
        rows = pl.ds(f * SIDE * ROW, SIDE * ROW)
        ref[rows, :] = ref[rows, :] + part(face, SIDE * ROW)
    elif r == 2:
        for a in range(SIDE):
            rows = pl.ds((a * SIDE + f) * ROW, ROW)
            ref[rows, :] = ref[rows, :] + part(face + ROW * a, ROW)
    elif r == 1:
        rows = pl.ds(f, SIDE * SIDE, ROW)
        ref[rows, :] = ref[rows, :] + part(face, SIDE * SIDE)
    elif r == 6:
        rows = pl.ds((f * SIDE + f) * ROW, ROW)
        ref[rows, :] = ref[rows, :] + part(edge, ROW)
    elif r == 5:
        rows = pl.ds(f * SIDE * ROW + f, SIDE, ROW)
        ref[rows, :] = ref[rows, :] + part(edge, SIDE)
    elif r == 3:
        rows = pl.ds(f * ROW + f, SIDE, SIDE * ROW)
        ref[rows, :] = ref[rows, :] + part(edge, SIDE)
    else:
        rows = pl.ds((f * SIDE + f) * ROW + f, 1)
        ref[rows, :] = ref[rows, :] + part(last, 1)


def put_faces(ref, put, r, side, face=FACE, edge=EDGE, last=LAST):
    f = PDEG * side
    if r == 4:
        put(face, SIDE * ROW, ref[pl.ds(f * SIDE * ROW, SIDE * ROW), :])
    elif r == 2:
        for a in range(SIDE):
            put(face + ROW * a, ROW, ref[pl.ds((a * SIDE + f) * ROW, ROW), :])
    elif r == 1:
        put(face, SIDE * SIDE, ref[pl.ds(f, SIDE * SIDE, ROW), :])
    elif r == 6:
        put(edge, ROW, ref[pl.ds((f * SIDE + f) * ROW, ROW), :])
    elif r == 5:
        put(edge, SIDE, ref[pl.ds(f * SIDE * ROW + f, SIDE, ROW), :])
    elif r == 3:
        put(edge, SIDE, ref[pl.ds(f * ROW + f, SIDE, SIDE * ROW), :])
    else:
        put(last, 1, ref[pl.ds((f * SIDE + f) * ROW + f, 1), :])


def loader(ref, slot):
    return lambda first, rows: ref[slot, pl.ds(first, rows), :]


def storer(ref, slot):
    def put(first, rows, value):
        ref[slot, pl.ds(first, rows), :] = value

    return put


def dot(a, b):
    if INTERPRET:
        a, b = a.astype(jnp.float32), b.astype(jnp.float32)
    return jnp.dot(a, b, preferred_element_type=jnp.float32)


def one_hot(mask):
    return mask.astype(jnp.float32).astype(jnp.bfloat16)


def mirror_in(me, perm_ref):
    row = lax.broadcasted_iota(jnp.int32, (NODES, NODES), 0)
    return one_hot(row == perm_ref[pl.ds(me, 1), :])


def open_kernel(
    me_ref, proj_ref, wave_ref, perm_ref, corner_ref, lane_ref, beta_ref, turned_ref, y_ref, p_ref, sx_ref, sy_ref, t_ref
):
    me = me_ref[0]
    t_ref[...] = jnp.zeros_like(t_ref)
    for a in range(SIDE):
        for b in range(SIDE):
            t_ref[pl.ds((a * SIDE + b) * ROW, SIDE), :] = wave_ref[a, b].astype(jnp.float32)
    y_ref[...] = dot(mirror_in(me, perm_ref), t_ref[...].astype(jnp.bfloat16)).astype(jnp.bfloat16)
    flat = proj_ref[...].reshape(CP, proj_ref.shape[2])
    spread = one_hot(lax.broadcasted_iota(jnp.int32, (flat.shape[1], NODES), 0) == perm_ref[pl.ds(8 + me, 1), :])
    order = one_hot(lax.broadcasted_iota(jnp.int32, (CP, CP), 0) == corner_ref[pl.ds(me, 1), :])
    ordered = dot(order, flat).astype(jnp.bfloat16)
    beta_ref[...] = dot(ordered, spread).astype(jnp.bfloat16)
    p_ref[...] = dot(beta_ref[...], y_ref[...])
    same = one_hot(lax.broadcasted_iota(jnp.int32, (NODES, NODES), 0) == lax.broadcasted_iota(jnp.int32, (NODES, NODES), 1))
    turned_ref[...] = dot_nt(same, beta_ref[...]).astype(jnp.bfloat16)
    row = lax.broadcasted_iota(jnp.int32, (NODES, 128), 0)
    zeros = jnp.zeros((FACE, W), jnp.float32)
    sx_ref[me] = jnp.zeros((2 * FACE, W), jnp.float32)
    sy_ref[7 - me] = zeros
    for r in range(1, 8):
        slot = me ^ r
        for first, at, rows in runs(shared(r, 1)):
            sx_ref[slot, pl.ds(first, rows), :] = p_ref[pl.ds(at, rows), :]
        used = NP * len(shared(r, 1))
        if used < FACE:
            sx_ref[slot, pl.ds(used, FACE - used), :] = jnp.zeros((FACE - used, W), jnp.float32)
        for base, out_ref, to, first in ((0, sx_ref, slot, FACE), (16, sy_ref, (7 - me) ^ r, 0)):
            low = one_hot(row == lane_ref[pl.ds(base + r, 1), :])
            high = one_hot(row == lane_ref[pl.ds(base + 8 + r, 1), :])
            packed = dot(beta_ref[pl.ds(0, FACE), :], low) + dot(beta_ref[pl.ds(FACE, FACE), :], high)
            out_ref[to, pl.ds(first, FACE), :] = packed


def dot_nt(a, b):
    if INTERPRET:
        a, b = a.astype(jnp.float32), b.astype(jnp.float32)
    return lax.dot_general(a, b, (((1,), (1,)), ((), ())), preferred_element_type=jnp.float32)


def dot_tn(a, b):
    if INTERPRET:
        a, b = a.astype(jnp.float32), b.astype(jnp.float32)
    return lax.dot_general(a, b, (((0,), (0,)), ((), ())), preferred_element_type=jnp.float32)


def chosen(table_ref, s, at, rows):
    pick = lax.broadcasted_iota(jnp.int32, (rows, ROWS), 0) + at
    return one_hot(pick == table_ref[pl.ds(s, 1), :])


def assemble_rows_kernel(
    first, me_ref, in_ref, beta_ref, lane_ref, table_ref, own_ref, far_ref, acc_ref, pick_ref, spread_ref
):
    me = me_ref[0]
    node = lax.broadcasted_iota(jnp.int32, (NODES, 128), 0)
    pick_ref[pl.ds(0, CP), :] = chosen(table_ref, 0, 0, CP)
    spread_ref[pl.ds(0, CP), :] = beta_ref[...].astype(jnp.float32)
    for s in range(1, 8):
        pick_ref[pl.ds(CP * s, CP), :] = chosen(table_ref, s, 0, CP)
        packed = in_ref[me ^ s, pl.ds(first, FACE), :].astype(jnp.bfloat16)
        for half in range(2):
            spread = one_hot(node == lane_ref[pl.ds(8 * half + s, 1), :])
            spread_ref[pl.ds(CP * s + FACE * half, FACE), :] = dot_nt(packed, spread)
    acc_ref[...] = dot_tn(pick_ref[...], spread_ref[...].astype(jnp.bfloat16))
    for r in range(1, 8):
        touched = (node == lane_ref[pl.ds(r, 1), :]).astype(jnp.float32)
        mask = 1.0 - lax.dot_general(
            jnp.ones((8, 128), jnp.float32), touched, (((1,), (1,)), ((), ())), preferred_element_type=jnp.float32
        )
        block = acc_ref[pl.ds((r - 1) * CHUNK, CHUNK), :] * mask[0:1, :]
        far_ref[pl.ds((r - 1) * CHUNK, CHUNK), :] = block.astype(jnp.bfloat16)
    own_ref[...] = acc_ref[pl.ds(FAR, CP), :].astype(jnp.bfloat16)


def assemble_columns_kernel(first, me_ref, in_ref, beta_ref, lane_ref, table_ref, own_ref, far_ref, acc_ref):
    me = 7 - me_ref[0]
    node = lax.broadcasted_iota(jnp.int32, (NODES, 128), 0)
    acc_ref[...] = dot(beta_ref[...], chosen(table_ref, 8, 0, CP))
    for s in range(1, 8):
        packed = in_ref[me ^ s, pl.ds(first, FACE), :].astype(jnp.bfloat16)
        for half in range(2):
            spread = one_hot(node == lane_ref[pl.ds(16 + 8 * half + s, 1), :])
            part = dot_nt(spread, packed).astype(jnp.bfloat16)
            acc_ref[...] = acc_ref[...] + dot(part, chosen(table_ref, 8 + s, FACE * half, FACE))
    for r in range(1, 8):
        touched = (node == lane_ref[pl.ds(16 + r, 1), :]).astype(jnp.float32)
        block = acc_ref[:, pl.ds((r - 1) * CHUNK, CHUNK)] * (1.0 - jnp.sum(touched, axis=1, keepdims=True))
        far_ref[:, pl.ds((r - 1) * CHUNK, CHUNK)] = block.astype(jnp.bfloat16)
    own_ref[...] = acc_ref[:, pl.ds(FAR, CP)].astype(jnp.bfloat16)


def send_terms(me, corr_ref, coupling_ref, ham_ref, y, own_ref, c_ref, f_ref, send_ref):
    c_ref[...] = jnp.dot(
        coupling_ref[...], corr_ref[...], precision=lax.Precision.HIGHEST, preferred_element_type=jnp.float32
    )
    f_ref[...] = dot(ham_ref[...], y) + dot(own_ref[...], c_ref[...].astype(jnp.bfloat16))
    send_ref[me] = jnp.zeros((CHUNK, W), jnp.float32)
    for r in range(1, 8):
        slot = me ^ r
        corners = near(r, 0)
        used = NP * len(corners)
        if used != FACE:
            send_ref[slot, pl.ds(used // 8 * 8, CHUNK - used // 8 * 8), :] = jnp.zeros(
                (CHUNK - used // 8 * 8, W), jnp.float32
            )
        for first, at, rows in runs(corners):
            send_ref[slot, pl.ds(first, rows), :] = c_ref[pl.ds(at, rows), :]
        if r == 1:
            send_ref[slot, pl.ds(FACE + 48, 8), :] = jnp.zeros((8, W), jnp.float32)
        put_faces(f_ref, storer(send_ref, slot), r, 0)


def first_kernel(me_ref, in_ref, p_ref, y_ref, coupling_ref, ham_ref, own_ref, f_ref, send_ref, corr_ref, c_ref):
    me = me_ref[0]
    corr_ref[...] = p_ref[...]
    for r in range(1, 8):
        for first, at, rows in runs(shared(r, 1)):
            corr_ref[pl.ds(at, rows), :] = corr_ref[pl.ds(at, rows), :] + in_ref[me ^ r, pl.ds(first, rows), :]
    send_terms(7 - me, corr_ref, coupling_ref, ham_ref, y_ref[...], own_ref, c_ref, f_ref, send_ref)


def vertex_kernel(
    me_ref, in_ref, z_ref, ownx_ref, coupling_ref, ham_ref, owny_ref, y_ref, f_ref, send_ref, t_ref, corr_ref, c_ref
):
    me = me_ref[0]
    t_ref[...] = z_ref[...]
    for r in range(1, 8):
        add_faces(t_ref, loader(in_ref, me ^ r), r, 1)
    y = t_ref[...].astype(jnp.bfloat16)
    y_ref[...] = y
    corr_ref[...] = dot(ownx_ref[...], y)
    for r in range(1, 8):
        for first, at, rows in runs(near(r, 1)):
            corr_ref[pl.ds(at, rows), :] = corr_ref[pl.ds(at, rows), :] + in_ref[me ^ r, pl.ds(first, rows), :]
    send_terms(7 - me, corr_ref, coupling_ref, ham_ref, y, owny_ref, c_ref, f_ref, send_ref)


def node_kernel(scales, final, me_ref, in_ref, f_ref, fary_ref, y_ref, before_ref, share_ref, farx_ref, z_ref, send_ref, a_ref, t_ref):
    me = me_ref[0]
    for r in range(1, 8):
        a_ref[pl.ds((r - 1) * CHUNK, CHUNK), :] = in_ref[(7 - me) ^ r].astype(jnp.bfloat16)
    t_ref[...] = f_ref[...] + dot(fary_ref[...], a_ref[...])
    for r in range(1, 8):
        add_faces(t_ref, loader(in_ref, (7 - me) ^ r), r, 0)
    applied, now, before = scales
    kept = now * y_ref[...].astype(jnp.float32)
    if before:
        kept = kept + before * before_ref[...].astype(jnp.float32)
    z_ref[...] = applied * t_ref[...] + share_ref[...] * kept
    if final:
        send_ref[...] = jnp.zeros_like(send_ref)
        for r in range(1, 8):
            put_faces(z_ref, storer(send_ref, me ^ r), r, 1, 0, 0, 0)
        return
    z = z_ref[...].astype(jnp.bfloat16)
    send_ref[me] = jnp.zeros((CHUNK, W), jnp.float32)
    for r in range(1, 8):
        send_ref[me ^ r] = dot(farx_ref[pl.ds((r - 1) * CHUNK, CHUNK), :], z)
        put_faces(z_ref, storer(send_ref, me ^ r), r, 1)


def close_kernel(me_ref, in_ref, z_ref, perm_ref, out_ref, t_ref):
    me = me_ref[0]
    t_ref[...] = z_ref[...]
    for r in range(1, 8):
        add_faces(t_ref, loader(in_ref, me ^ r), r, 1, 0, 0, 0)
    y = dot(mirror_in(me, perm_ref), t_ref[...].astype(jnp.bfloat16))
    for a in range(SIDE):
        for b in range(SIDE):
            first = (a * SIDE + b) * ROW
            out_ref[a, b] = y[first : first + SIDE].astype(jnp.bfloat16)


def call(kernel, me, inputs, outs, scratch=(), limit=LIMIT):
    smem = pl.BlockSpec(memory_space=pltpu.SMEM)
    vmem = pl.BlockSpec(memory_space=pltpu.VMEM)
    return pl.pallas_call(
        kernel,
        out_shape=[jax.ShapeDtypeStruct(shape, dtype) for shape, dtype in outs],
        in_specs=[smem] + [vmem] * len(inputs),
        out_specs=[vmem] * len(outs),
        scratch_shapes=[pltpu.VMEM(shape, dtype) for shape, dtype in scratch],
        compiler_params=pltpu.CompilerParams(vmem_limit_bytes=limit),
        interpret=INTERPRET,
    )(me, *inputs)


def mirrored(values, flips):
    for d in range(3):
        values = jnp.where(flips[d], jnp.flip(values, d), values)
    return values


def exact_dot(a, b, dims):
    return lax.dot_general(a, b, (dims, ((), ())), preferred_element_type=jnp.float32).astype(a.dtype)


def local(wavefunctions, cell_hamiltonian, projectors, atom_species, coupling):
    node_count = cell_hamiltonian.shape[3]
    sizes = [lax.axis_size(axis) for axis in AXES]
    bits = [(lax.axis_index(axis) + sizes[d] - OFFSETS[1][d]) % 2 for d, axis in enumerate(AXES)]
    flips = [bit == 1 for bit in bits]
    me = (4 * bits[0] + 2 * bits[1] + bits[2]).astype(jnp.int32).reshape(1)

    def mirror_of(shape, padded_dim):
        padded = lax.broadcasted_iota(jnp.int32, shape, padded_dim)
        plain = lax.broadcasted_iota(jnp.int32, shape, 1 - padded_dim)
        place = [padded // (SIDE * ROW), (padded // ROW) % SIDE, padded % ROW]
        inside = place[2] < SIDE
        place = [jnp.where(f, PDEG - p, p) for f, p in zip(flips, place)]
        same = plain == (place[0] * SIDE + place[1]) * SIDE + place[2]
        return jnp.logical_and(same, inside).astype(jnp.bfloat16)

    into = mirror_of((NODES, node_count), 0)
    back = mirror_of((node_count, NODES), 1)
    ham = exact_dot(into, cell_hamiltonian.reshape(node_count, node_count), ((1,), (0,)))
    ham = exact_dot(ham, back, ((1,), (0,)))
    species = mirrored(atom_species, flips).reshape(8)
    kinds = jnp.arange(1, coupling.shape[0] + 1, dtype=jnp.int32)
    mask = (species[:, None] == kinds).astype(jnp.float32)
    per_corner = jnp.einsum("vs,spq->vpq", mask, coupling, precision=lax.Precision.HIGHEST)
    blocks = jnp.tile(per_corner.reshape(CP, NP), (1, 8))
    corner_of = jnp.arange(CP) // NP
    blocks = jnp.where(corner_of[:, None] == corner_of[None, :], blocks, 0.0)

    f32, bf16 = jnp.float32, jnp.bfloat16
    lanes = np.concatenate([*lane_tables(1), *lane_tables(0)])
    tables = np.concatenate([corner_table(1), corner_table(0)])
    perm, corner = mirror_tables()
    by_row = jnp.transpose(projectors.reshape(8, NP, node_count), (1, 0, 2))
    plane = (NODES, W)
    betas, turned, current, p, sx, sy = call(
        open_kernel,
        me,
        (by_row, wavefunctions, perm, corner, lanes),
        [
            ((CP, NODES), bf16),
            ((NODES, CP), bf16),
            (plane, bf16),
            ((CP, W), f32),
            ((8, 2 * FACE, W), f32),
            ((8, FACE, W), f32),
        ],
        [(plane, f32)],
        58 << 20,
    )
    ax = swap(sx, 1)
    ay = swap(sy, 0)
    ownx, farx = call(
        functools.partial(assemble_rows_kernel, FACE),
        me,
        (ax, betas, lanes, tables),
        [((CP, NODES), bf16), ((FAR, NODES), bf16)],
        [((ROWS, NODES), f32), ((8 * CP, ROWS), bf16), ((8 * CP, NODES), f32)],
        24 << 20,
    )
    owny, fary = call(
        functools.partial(assemble_columns_kernel, 0),
        me,
        (ay, turned, lanes, tables),
        [((NODES, CP), bf16), ((NODES, FAR), bf16)],
        [((NODES, ROWS), f32)],
    )

    node = np.arange(NODES)
    place = [node // (SIDE * ROW), (node // ROW) % SIDE, node % ROW]
    share = np.prod([np.where(q == PDEG, 0.5, 1.0) for q in place], axis=0).astype(np.float32).reshape(NODES, 1)

    packet = ((8, CHUNK, W), f32)
    f, send = call(
        first_kernel, me, (ax, p, current, blocks, ham, owny), [(plane, f32), packet], [((CP, W), f32)] * 2
    )
    previous = current
    for step in range(ORDER):
        final = step == ORDER - 1
        arrived = swap(send, 0)
        scales = (1.0 / HALF, -CENTER / HALF, 0.0) if step == 0 else (2.0 / HALF, -2.0 * CENTER / HALF, -1.0)
        z, send = call(
            functools.partial(node_kernel, scales, final),
            me,
            (arrived, f, fary, current, previous, share, farx),
            [(plane, f32), ((8, 56, W), f32) if final else packet],
            [((7 * CHUNK, W), bf16), (plane, f32)],
        )
        arrived = swap(send, 1)
        if final:
            (out,) = call(close_kernel, me, (arrived, z, perm), [(wavefunctions.shape, bf16)], [(plane, f32)])
            return out
        previous = current
        current, f, send = call(
            vertex_kernel,
            me,
            (arrived, z, ownx, blocks, ham, owny),
            [(plane, bf16), (plane, f32), packet],
            [(plane, f32), ((CP, W), f32), ((CP, W), f32)],
        )


def solution(mesh):
    placed = (
        P("gx", "gy", "gz", None),
        P("gx", "gy", "gz", None, None),
        P("gx", "gy", "gz", None, None, None),
        P("gx", "gy", "gz"),
        P(),
    )
    return jax.shard_map(
        local, mesh=mesh, in_specs=placed, out_specs=P("gx", "gy", "gz", None), check_vma=False
    )
```
